32 devices in a mesh: sy: 8 (over z, y), sx: 4 (over x, core).
Axes of the slice: x: 2, y: 2, z: 4, core: 2. Of those that a mesh axis runs over, the one named last changes fastest.
Arguments:
- object_re: float32 [2048, 1024], P('sy', 'sx'), may hold values from -6 to 6
- object_im: float32 [2048, 1024], P('sy', 'sx'), may hold values from -6 to 6
- probe_re: float32 [2, 256, 256], replicated, may hold values from -6 to 6
- probe_im: float32 [2, 256, 256], replicated, may hold values from -6 to 6
- amplitudes: float32 [8, 4, 8, 256, 256], P('sy', 'sx'), may hold values from 0.5 to 3
- offsets: int32 [8, 4, 8, 2], P('sy', 'sx'), may hold values from -128 to 127
- visit_order: int32 [8, 4, 8], P('sy', 'sx'), may hold values from 0 to 7, each once within a row
Outputs:
- object_new_re: float32 [2048, 1024], P('sy', 'sx')
- object_new_im: float32 [2048, 1024], P('sy', 'sx')
- probe_new_re: float32 [2, 256, 256], replicated
- probe_new_im: float32 [2, 256, 256], replicated
The draws below stay inside these ranges and needn't reach their ends.
Inputs may be any that keep to these rules, and one draw needn't show every extreme that they name: `visit_order`: each tile's entries are a permutation of 0 to 7.
All inputs are finite; a program needn't handle non-finite values.
Results may differ from the reference program's by a relative error of at most 0.0019.
Values sent between devices are 32-bit elements; how exact they have to be, the bound alone decides.
No kernel may reach another device: no remote copies, remote signals or barrier semaphores. Data moves between devices by JAX's collectives and lax.ppermute only.
A program may use at most 64 MiB of HBM per device.

```python
import math
import jax
import jax.numpy as jnp
from jax import lax

FRAME = 256
MODES = 2
POS_DEV = 8
BATCHES = 2
TILE = 256
HALO = 128
TILE_ROWS = 8
TILE_COLS = 4
NY = 2048
NX = 1024
N_SY = 8
N_SX = 4


def place_ends(values, own_key, low, top_value):
    shape = values.shape
    spot = [jax.random.randint(jax.random.fold_in(own_key, axis), (), 0, shape[axis]) for axis in range(len(shape))]
    values = values.at[tuple(spot)].set(low)
    longest = shape.index(max(shape))
    spot[longest] = (spot[longest] + 1) % shape[longest]
    return values.at[tuple(spot)].set(top_value)


def levels(own_key, shape, split, low, high):
    gain, own = 1.0, jax.random.fold_in(own_key, 6)
    for dim, shards_of in split:
        heights = jnp.exp(jax.random.uniform(jax.random.fold_in(own, dim), (shards_of,), jnp.float32, low / len(split), high / len(split)))
        gain = gain * jnp.repeat(heights, shape[dim] // shards_of).reshape([-1 if axis == dim else 1 for axis in range(len(shape))])
    return gain


def noise(own_key, shape, spread, bound, shards=(), held_as=jnp.bfloat16):
    result = jax.random.normal(own_key, shape, jnp.float32) * spread
    if len(shards) > 0:
        result = levels(own_key, shape, shards, -0.22, 0.18) * result
    return jnp.clip(result, min=-bound, max=bound).astype(held_as)


def setup_inputs(seed: int = 0) -> dict:
    seeds = jax.random.split(jax.random.key(seed), 8)
    object_re = noise(seeds[0], (NY, NX), 1.0, 6.0, ((0, 8), (1, 4)), jnp.float32)
    object_im = noise(seeds[1], (NY, NX), 1.0, 6.0, ((0, 8), (1, 4)), jnp.float32)
    probe_re = noise(seeds[2], (MODES, FRAME, FRAME), 1.0, 6.0, (), jnp.float32)
    probe_im = noise(seeds[3], (MODES, FRAME, FRAME), 1.0, 6.0, (), jnp.float32)
    amplitudes = jnp.clip(0.5 + 2.5 * jax.random.uniform(seeds[4], (TILE_ROWS, TILE_COLS, POS_DEV, FRAME, FRAME), jnp.float32) ** levels(seeds[4], (TILE_ROWS, TILE_COLS, POS_DEV, FRAME, FRAME), ((0, 8), (1, 4)), -0.2, 0.2), 0.5, 3.0)
    offsets = place_ends(jax.random.randint(seeds[5], (TILE_ROWS, TILE_COLS, POS_DEV, 2), -HALO, HALO), jax.random.fold_in(seeds[5], 1), -HALO, HALO - 1).astype(jnp.int32)
    visit_order = jax.vmap(lambda own: jax.random.permutation(own, POS_DEV))(jax.random.split(seeds[6], TILE_ROWS * TILE_COLS)).reshape((TILE_ROWS, TILE_COLS, POS_DEV)).astype(jnp.int32)
    return {"object_re": object_re, "object_im": object_im, "probe_re": probe_re, "probe_im": probe_im, "amplitudes": amplitudes, "offsets": offsets, "visit_order": visit_order}


OBJECT_RATE = 0.25
PROBE_GAIN = 4.0

def dft_tables(frame_size):
    ramp_values = jnp.arange(frame_size, dtype=jnp.int32)
    product = ramp_values[:, None] * ramp_values[None, :] % frame_size
    phase_angle = 2.0 * math.pi / frame_size * product.astype(jnp.float32)
    norm_scale = 1.0 / math.sqrt(frame_size)
    table_re = (jnp.cos(phase_angle) * norm_scale).astype(jnp.bfloat16)
    table_im = (-jnp.sin(phase_angle) * norm_scale).astype(jnp.bfloat16)
    return (table_re, table_im)

def left_product(matrix, values_in):
    return jnp.einsum('jk,bmkl->bmjl', matrix.astype(jnp.float32), values_in.astype(jnp.float32))

def right_product(values_in, matrix):
    return jnp.einsum('bmjk,kl->bmjl', values_in.astype(jnp.float32), matrix.astype(jnp.float32))

def transform(real_part, imag_part, table_re, table_im):
    half_re = (left_product(table_re, real_part) - left_product(table_im, imag_part)).astype(jnp.bfloat16)
    half_im = (left_product(table_re, imag_part) + left_product(table_im, real_part)).astype(jnp.bfloat16)
    far_re = right_product(half_re, table_re) - right_product(half_im, table_im)
    far_im = right_product(half_im, table_re) + right_product(half_re, table_im)
    return (far_re, far_im)

def correct(patch_re, patch_im, chosen_amps, probe_re, probe_im, table_re, table_im):
    exit_re = (probe_re[None] * patch_re[:, None] - probe_im[None] * patch_im[:, None]).astype(jnp.bfloat16)
    exit_im = (probe_re[None] * patch_im[:, None] + probe_im[None] * patch_re[:, None]).astype(jnp.bfloat16)
    far_re, far_im = transform(exit_re, exit_im, table_re, table_im)
    intensity = lax.optimization_barrier(jnp.sum(far_re * far_re + far_im * far_im, axis=1))
    amp_ratio = chosen_amps / jnp.sqrt(jnp.maximum(intensity, 1.0))
    fixed_re = (far_re * amp_ratio[:, None]).astype(jnp.bfloat16)
    fixed_im = (far_im * amp_ratio[:, None]).astype(jnp.bfloat16)
    back_re, back_im = transform(fixed_re, fixed_im, table_re, -table_im)
    delta_re = back_re - exit_re.astype(jnp.float32)
    delta_im = back_im - exit_im.astype(jnp.float32)
    object_grad_re = lax.optimization_barrier(jnp.sum(probe_re[None] * delta_re + probe_im[None] * delta_im, axis=1))
    object_grad_im = lax.optimization_barrier(jnp.sum(probe_re[None] * delta_im - probe_im[None] * delta_re, axis=1))
    probe_grad_re = lax.optimization_barrier(jnp.sum(patch_re[:, None] * delta_re + patch_im[:, None] * delta_im, axis=0))
    probe_grad_im = lax.optimization_barrier(jnp.sum(patch_re[:, None] * delta_im - patch_im[:, None] * delta_re, axis=0))
    return (object_grad_re, object_grad_im, probe_grad_re, probe_grad_im)

def reference(object_re, object_im, probe_re, probe_im, amplitudes, offsets, visit_order):
    table_re, table_im = dft_tables(FRAME)
    tile_count = N_SY * N_SX
    batch_size = POS_DEV // BATCHES
    amp_flat = amplitudes.reshape(tile_count, POS_DEV, FRAME, FRAME)
    offset_flat = offsets.reshape(tile_count, POS_DEV, 2)
    order_flat = visit_order.reshape(tile_count, POS_DEV)
    probe_power = jnp.max(lax.optimization_barrier(jnp.sum(probe_re * probe_re + probe_im * probe_im, axis=0)))
    object_pair = jnp.pad(jnp.stack([object_re, object_im]), ((0, 0), (HALO, HALO), (HALO, HALO)))
    grad_re = jnp.zeros((MODES, FRAME, FRAME), jnp.float32)
    grad_im = jnp.zeros((MODES, FRAME, FRAME), jnp.float32)
    for batch_index in range(BATCHES):

        def one_tile(tile_index, loop_state):
            accum, probe_acc_re, probe_acc_im = loop_state
            tile_row = (tile_index // N_SX).astype(jnp.int32)
            tile_col = (tile_index % N_SX).astype(jnp.int32)
            order_row = lax.dynamic_index_in_dim(order_flat, tile_index, 0, keepdims=False)
            chosen = order_row[batch_index * batch_size:(batch_index + 1) * batch_size]
            offset_row = lax.dynamic_index_in_dim(offset_flat, tile_index, 0, keepdims=False)
            amp_row = lax.dynamic_index_in_dim(amp_flat, tile_index, 0, keepdims=False)
            chosen_offsets = offset_row[chosen]
            chosen_amps = amp_row[chosen]
            top_rows = (tile_row * TILE + chosen_offsets[:, 0] + HALO).astype(jnp.int32)
            left_cols = (tile_col * TILE + chosen_offsets[:, 1] + HALO).astype(jnp.int32)
            patches = jax.vmap(lambda top_index, left_index: lax.dynamic_slice(object_pair, (jnp.int32(0), top_index, left_index), (2, FRAME, FRAME)))(top_rows, left_cols)
            obj_re, obj_im, part_re, part_im = correct(patches[:, 0], patches[:, 1], chosen_amps, probe_re, probe_im, table_re, table_im)
            update_terms = jnp.stack([obj_re, obj_im], axis=1)
            for member in range(batch_size):
                start_at = (jnp.int32(0), top_rows[member], left_cols[member])
                current = lax.dynamic_slice(accum, start_at, (2, FRAME, FRAME))
                accum = lax.dynamic_update_slice(accum, current + update_terms[member], start_at)
            return (accum, probe_acc_re + part_re, probe_acc_im + part_im)
        accum, grad_re, grad_im = lax.fori_loop(0, tile_count, one_tile, (jnp.zeros_like(object_pair), grad_re, grad_im))
        inner = object_pair[:, HALO:-HALO, HALO:-HALO] + OBJECT_RATE * accum[:, HALO:-HALO, HALO:-HALO] / probe_power
        object_pair = jnp.pad(inner, ((0, 0), (HALO, HALO), (HALO, HALO)))
    probe_rate = PROBE_GAIN / (POS_DEV * math.sqrt(N_SY * N_SX))
    final = object_pair[:, HALO:-HALO, HALO:-HALO]
    return (final[0], final[1], probe_re + probe_rate * grad_re, probe_im + probe_rate * grad_im)
```

```python
import functools
import math

import jax
import jax.numpy as jnp
from jax import lax
from jax.experimental import pallas as pl
from jax.experimental.pallas import tpu as pltpu
from jax.sharding import PartitionSpec as P

BATCHES = 2

OBJECT_RATE = 0.25
PROBE_GAIN = 4.0

VMEM = pl.BlockSpec(memory_space=pltpu.VMEM)
SMEM = pl.BlockSpec(memory_space=pltpu.SMEM)
ANY = pl.BlockSpec(memory_space=pl.ANY)


def f32(*shape):
    return jax.ShapeDtypeStruct(shape, jnp.float32)


def dft_tables(frame_size):
    ramp_values = jnp.arange(frame_size, dtype=jnp.int32)
    product = ramp_values[:, None] * ramp_values[None, :] % frame_size
    phase_angle = 2.0 * math.pi / frame_size * product.astype(jnp.float32)
    norm_scale = 1.0 / math.sqrt(frame_size)
    table_re = (jnp.cos(phase_angle) * norm_scale).astype(jnp.bfloat16)
    table_im = (-jnp.sin(phase_angle) * norm_scale).astype(jnp.bfloat16)
    return (table_re, table_im)


def pair_exchange(block, axis, odd):
    count = lax.axis_size(axis)
    perm = []
    for low in range(odd, count - 1, 2):
        perm += [(low, low + 1), (low + 1, low)]
    return lax.ppermute(block, axis, perm)


def exchange_both(even_block, odd_block, axis):
    return pair_exchange(even_block, axis, 0), pair_exchange(odd_block, axis, 1)


def parity(axis):
    return lax.rem(lax.axis_index(axis), 2)


def aligned(value, unit):
    return pl.multiple_of(value, unit)


def pack_tile_kernel(h, obj_re, obj_im, y_even, y_odd, x_even, x_odd):
    py, px = parity("sy"), parity("sx")
    for c, obj in enumerate((obj_re, obj_im)):
        for lb in range(2):
            cols = pl.ds(lb * h, h)
            y_even[c, lb] = obj[pl.ds(aligned((1 - py) * h, h), h), cols]
            y_odd[c, lb] = obj[pl.ds(aligned(py * h, h), h), cols]
        x_even[c] = obj[:, pl.ds(aligned((1 - px) * h, h), h)]
        x_odd[c] = obj[:, pl.ds(aligned(px * h, h), h)]


def pack_corner_kernel(up_even, up_odd, c_even, c_odd):
    px = parity("sx")
    for side, strip in enumerate((up_even, up_odd)):
        for c in range(2):
            c_even[side, c] = strip[c, 1 - px]
            c_odd[side, c] = strip[c, px]


def batch_body(batch, size, order, offs, probe_re, probe_im, table_left, table_right, amp_hbm, ext, accum, grads, scratch):
    amp, patch, exits, fixed, mixed, field, amp_sems = scratch
    f = probe_re.shape[1]
    h = f // 2
    rows = 32
    probe = (probe_re, probe_im)

    def amp_copy(j):
        chosen = order[0, 0, batch * size + j]
        return pltpu.make_async_copy(amp_hbm.at[0, 0, chosen], amp.at[j], amp_sems.at[j])

    for j in range(size):
        amp_copy(j).start()
    accum[...] = jnp.zeros_like(accum)
    lane = lax.broadcasted_iota(jnp.int32, (rows, h), 1)

    def left_side(table, values):
        for c in range(2):
            product = jnp.dot(table[pl.ds(c * f, f), :], values[...], preferred_element_type=jnp.float32)
            for m in range(2):
                mixed[pl.ds(m * f, f), pl.ds(c * f, f)] = product[:, m * f : (m + 1) * f].astype(jnp.bfloat16)

    def right_side(table):
        field[...] = jnp.dot(mixed[...], table[...], preferred_element_type=jnp.float32)

    @pl.loop(0, size)
    def _(j):
        chosen = order[0, 0, batch * size + j]
        top = offs[0, 0, chosen, 0] + h
        left = offs[0, 0, chosen, 1] + h
        first = lax.div(left, h)
        shift = lax.rem(left, h)
        back_shift = lax.rem(h - shift, h)
        inside = lane < h - shift
        for r in range(0, f, rows):
            here = pl.ds(r, rows)
            window = []
            for c in range(2):
                a, b, d = [
                    pltpu.roll(ext[c, first + k, pl.ds(top + r, rows), :], back_shift, 1) for k in range(3)
                ]
                window.append([jnp.where(inside, a, b), jnp.where(inside, b, d)])
            for lb in range(2):
                o_re, o_im = window[0][lb], window[1][lb]
                patch[0, here, pl.ds(lb * h, h)] = o_re
                patch[1, here, pl.ds(lb * h, h)] = o_im
                for m in range(2):
                    p_re, p_im = [part[m, here, pl.ds(lb * h, h)] for part in probe]
                    spot = pl.ds(m * f + lb * h, h)
                    exits[pl.ds(r, rows), spot] = (p_re * o_re - p_im * o_im).astype(jnp.bfloat16)
                    exits[pl.ds(f + r, rows), spot] = (p_re * o_im + p_im * o_re).astype(jnp.bfloat16)
        left_side(table_left, exits)
        right_side(table_right)
        amp_copy(j).wait()
        for r in range(0, f, rows):
            for lb in range(2):
                far = [
                    [field[pl.ds(m * f + r, rows), pl.ds(c * f + lb * h, h)] for c in range(2)] for m in range(2)
                ]
                power = sum(part * part for mode in far for part in mode)
                ratio = amp[j, pl.ds(r, rows), pl.ds(lb * h, h)] * lax.rsqrt(jnp.maximum(power, 1.0))
                for m in range(2):
                    for c in range(2):
                        spot = pl.ds(m * f + lb * h, h)
                        fixed[pl.ds(c * f + r, rows), spot] = (far[m][c] * ratio).astype(jnp.bfloat16)
        left_side(table_right, fixed)
        right_side(table_left)
        beyond = lane >= shift
        for r in range(0, f, rows):
            here = pl.ds(r, rows)
            term = [[0.0, 0.0], [0.0, 0.0]]
            for lb in range(2):
                cols = pl.ds(lb * h, h)
                o_re, o_im = patch[0, here, cols], patch[1, here, cols]
                for m in range(2):
                    d_re, d_im = [
                        field[pl.ds(m * f + r, rows), pl.ds(c * f + lb * h, h)]
                        - exits[pl.ds(c * f + r, rows), pl.ds(m * f + lb * h, h)].astype(jnp.float32)
                        for c in range(2)
                    ]
                    p_re, p_im = [part[m, here, cols] for part in probe]
                    term[0][lb] += p_re * d_re + p_im * d_im
                    term[1][lb] += p_re * d_im - p_im * d_re
                    grads[m, 0, lb, here, :] += o_re * d_re + o_im * d_im
                    grads[m, 1, lb, here, :] += o_re * d_im - o_im * d_re
            for c in range(2):
                a, b = [pltpu.roll(part, shift, 1) for part in term[c]]
                there = pl.ds(top + r, rows)
                accum[c, first, there, :] += jnp.where(beyond, a, 0.0)
                accum[c, first + 1, there, :] += jnp.where(beyond, b, a)
                accum[c, first + 2, there, :] += jnp.where(beyond, 0.0, b)


def send_columns(h, accum, own, x_even, x_odd):
    px = parity("sx")
    for c in range(2):
        own[c] = accum[c, 1:3]
        x_even[c] = accum[c, (1 - px) * 3]
        x_odd[c] = accum[c, px * 3]


def first_batch_kernel(
    h, size, order, offs, obj_re, obj_im, up_even, up_odd, x_even, x_odd, c_even, c_odd,
    probe_re, probe_im, table_left, table_right, amp_hbm, own, send_even, send_odd, grads, ext, accum, *scratch,
):
    py, px = parity("sy"), parity("sx")
    rows_even, rows_odd = [pl.ds(aligned(side * 3 * h, h), h) for side in (1 - py, py)]
    cols_even, cols_odd = (1 - px) * 3, px * 3
    for c, obj in enumerate((obj_re, obj_im)):
        for lb in range(2):
            ext[c, 1 + lb, h : 3 * h] = obj[:, lb * h : (lb + 1) * h]
            ext[c, 1 + lb, rows_even] = up_even[c, lb]
            ext[c, 1 + lb, rows_odd] = up_odd[c, lb]
        for block, column, corner in ((cols_even, x_even, c_even), (cols_odd, x_odd, c_odd)):
            ext[c, block, h : 3 * h] = column[c]
            ext[c, block, rows_even] = corner[0, c]
            ext[c, block, rows_odd] = corner[1, c]
    grads[...] = jnp.zeros_like(grads)
    batch_body(0, size, order, offs, probe_re, probe_im, table_left, table_right, amp_hbm, ext, accum, grads, scratch)
    send_columns(h, accum, own, send_even, send_odd)


def later_batch_kernel(
    h, size, batch, last, order, offs, columns, x_even, x_odd, grads_in,
    probe_re, probe_im, table_left, table_right, amp_hbm, own, send_even, send_odd, *rest,
):
    outs, (ext, accum, grads, *scratch) = rest[: 2 if last else 1], rest[2 if last else 1 :]
    px = parity("sx")
    for c in range(2):
        ext[c, 1:3] = columns[c]
        ext[c, (1 - px) * 3] = x_even[c]
        ext[c, px * 3] = x_odd[c]
    grads[...] = grads_in[...]
    batch_body(batch, size, order, offs, probe_re, probe_im, table_left, table_right, amp_hbm, ext, accum, grads, scratch)
    send_columns(h, accum, own, send_even, send_odd)
    if last:
        keep, give = outs
        keep[...] = grads[px]
        give[...] = grads[1 - px]
    else:
        outs[0][...] = grads[...]


def batch_scratch(size, f, with_grads):
    h = f // 2
    return [
        pltpu.VMEM((2, 4, 4 * h, h), jnp.float32),
        pltpu.VMEM((2, 4, 4 * h, h), jnp.float32),
        *([pltpu.VMEM((2, 2, 2, f, h), jnp.float32)] if with_grads else []),
        pltpu.VMEM((size, f, f), jnp.float32),
        pltpu.VMEM((2, f, f), jnp.float32),
        pltpu.VMEM((2 * f, 2 * f), jnp.bfloat16),
        pltpu.VMEM((2 * f, 2 * f), jnp.bfloat16),
        pltpu.VMEM((2 * f, 2 * f), jnp.bfloat16),
        pltpu.VMEM((2 * f, 2 * f), jnp.float32),
        pltpu.SemaphoreType.DMA((size,)),
    ]


def fold_columns_kernel(h, own, x_even, x_odd, y_even, y_odd):
    py, px = parity("sy"), parity("sx")
    halves = [pl.ds(aligned(side * 2 * h, 2 * h), 2 * h) for side in (1 - py, py)]
    for c in range(2):
        for block, column in ((1 - px, x_even), (px, x_odd)):
            for half, out in zip(halves, (y_even, y_odd)):
                out[c, block] = own[c, block, half] + column[c, half]


def has_partner(axis, odd):
    index, count = lax.axis_index(axis), lax.axis_size(axis)
    lower = lax.rem(index, 2) == odd
    partner = jnp.where(lower, index + 1, index - 1)
    return (partner >= 0) & (partner < count)


def update_kernel(h, scale, y_even, y_odd, got_even, got_odd, obj_re, obj_im, up_even, up_odd, columns, x_even, x_odd):
    py, px = parity("sy"), parity("sx")
    rate = scale[0]
    for c, obj in enumerate((obj_re, obj_im)):
        for lb in range(2):
            for odd, side, mine, got, up in (
                (0, 1 - py, y_even, got_even, up_even),
                (1, py, y_odd, got_odd, up_odd),
            ):
                rate_halo = jnp.where(has_partner("sy", odd), rate, 0.0)
                inner, outer = [pl.ds(aligned(at * h, h), h) for at in (1 - side, side)]
                own_rows = pl.ds(aligned(side * h, h), h)
                total = mine[c, lb, inner] + got[c, lb, inner]
                columns[c, lb, pl.ds(aligned((1 + side) * h, h), h)] = obj[own_rows, lb * h : (lb + 1) * h] + rate * total
                total = mine[c, lb, outer] + got[c, lb, outer]
                columns[c, lb, pl.ds(aligned(side * 3 * h, h), h)] = up[c, lb] + rate_halo * total
        x_even[c] = columns[c, 1 - px]
        x_odd[c] = columns[c, px]


def fold_last_kernel(h, own, x_even, x_odd, inner, y_even, y_odd):
    py, px = parity("sy"), parity("sx")
    for c in range(2):
        for block, column in ((1 - px, x_even), (px, x_odd)):
            inner[c, block] = own[c, block, h : 3 * h] + column[c, h : 3 * h]
            for side, out in ((1 - py, y_even), (py, y_odd)):
                halo = pl.ds(aligned(side * 3 * h, h), h)
                out[c, block] = own[c, block, halo] + column[c, halo]


def finish_object_kernel(h, scale, inner, y_even, y_odd, columns, out_re, out_im):
    py = parity("sy")
    rate = scale[0]
    for c, out in enumerate((out_re, out_im)):
        for lb in range(2):
            for side, got in ((1 - py, y_even), (py, y_odd)):
                here = pl.ds(aligned(side * h, h), h)
                old = columns[c, lb, pl.ds(aligned((1 + side) * h, h), h)]
                out[here, lb * h : (lb + 1) * h] = old + rate * (inner[c, lb, here] + got[c, lb])


def plan_groups():
    bits = {axis: lax.axis_size(axis).bit_length() - 1 for axis in ("sy", "sx")}
    for axis, count in bits.items():
        if 1 << count != lax.axis_size(axis):
            raise ValueError("axis size")
    first, *rest = [("sx", bit) for bit in range(bits["sx"])]
    lower = [("sy", bit) for bit in range(bits["sy"])]
    queue = []
    while rest or lower:
        for line in (rest, lower):
            if line:
                queue.append(line.pop(0))
    return [[first]] + [queue[i : i + 2] for i in range(0, len(queue), 2)]


def group_index(group):
    return sum(((lax.axis_index(axis) >> bit) & 1) << spot for spot, (axis, bit) in enumerate(group))


def group_exchange(block, group, mask):
    count_y, count_x = lax.axis_size("sy"), lax.axis_size("sx")
    flip = {"sy": 0, "sx": 0}
    for spot, (axis, bit) in enumerate(group):
        flip[axis] |= ((mask >> spot) & 1) << bit
    perm = [
        (y * count_x + x, (y ^ flip["sy"]) * count_x + (x ^ flip["sx"])) for y in range(count_y) for x in range(count_x)
    ]
    return lax.ppermute(block, ("sy", "sx"), perm)


def sum_kernel(group, count, *refs):
    parts, outs = refs[:count], refs[count:]
    spot = group_index(group) if group else 0
    for mask, out in enumerate(outs):
        size = out.shape[0]
        piece = pl.ds(aligned((spot ^ mask) * size, size), size)
        out[...] = sum(part[piece, :] for part in parts)


def gather_kernel(group, *refs):
    parts, out = refs[:-1], refs[-1]
    spot = group_index(group)
    size = parts[0].shape[0]
    for mask, part in enumerate(parts):
        out[pl.ds(aligned((spot ^ mask) * size, size), size), :] = part[...]


def finish_probe_kernel(rate, keep, got, probe_re, probe_im, out_re, out_im):
    px = parity("sx")
    f = probe_re.shape[1]
    h = f // 2
    for mode, part in ((px, keep), (1 - px, got)):
        for c, (probe, out) in enumerate(((probe_re, out_re), (probe_im, out_im))):
            for lb in range(2):
                cols = slice(lb * h, (lb + 1) * h)
                out[mode, :, cols] = probe[mode, :, cols] + rate * part[c, lb]


def local(object_re, object_im, probe_re, probe_im, amplitudes, offsets, visit_order):
    f = probe_re.shape[1]
    h = f // 2
    positions = visit_order.shape[-1]
    size = positions // BATCHES
    table_re, table_im = dft_tables(f)
    table_left = jnp.block([[table_re, -table_im], [table_im, table_re]])
    table_right = jnp.block([[table_re, table_im], [-table_im, table_re]])
    probe_power = jnp.max(jnp.sum(probe_re * probe_re + probe_im * probe_im, axis=0))
    scale = (OBJECT_RATE / probe_power).reshape(1)

    strip = f32(2, 2, h, h)
    up = pl.pallas_call(
        functools.partial(pack_tile_kernel, h),
        out_shape=[strip, strip, f32(2, 2 * h, h), f32(2, 2 * h, h)],
        in_specs=[VMEM] * 2, out_specs=[VMEM] * 4, name="pack_tile",
    )(object_re, object_im)
    up_even, up_odd = exchange_both(up[0], up[1], "sy")
    x_even, x_odd = exchange_both(up[2], up[3], "sx")
    corners = pl.pallas_call(
        pack_corner_kernel, out_shape=[strip, strip], in_specs=[VMEM] * 2, out_specs=[VMEM] * 2, name="pack_corner",
    )(up_even, up_odd)
    c_even, c_odd = exchange_both(corners[0], corners[1], "sx")

    column = f32(2, 4 * h, h)
    own_type = f32(2, 2, 4 * h, h)
    grads_type = f32(2, 2, 2, f, h)
    params = pltpu.CompilerParams(vmem_limit_bytes=48 << 20)
    fixed_args = (probe_re, probe_im, table_left, table_right, amplitudes)
    fixed_specs = [VMEM] * 4 + [ANY]
    own, send_even, send_odd, grads = pl.pallas_call(
        functools.partial(first_batch_kernel, h, size),
        out_shape=[own_type, column, column, grads_type],
        in_specs=[SMEM] * 2 + [VMEM] * 8 + fixed_specs, out_specs=[VMEM] * 4,
        scratch_shapes=batch_scratch(size, f, False), compiler_params=params, name="batch_first",
    )(visit_order, offsets, object_re, object_im, up_even, up_odd, x_even, x_odd, c_even, c_odd, *fixed_args)

    x_even, x_odd = exchange_both(send_even, send_odd, "sx")
    half = f32(2, 2, 2 * h, h)
    y_even, y_odd = pl.pallas_call(
        functools.partial(fold_columns_kernel, h),
        out_shape=[half, half], in_specs=[VMEM] * 3, out_specs=[VMEM] * 2, name="fold_columns",
    )(own, x_even, x_odd)
    got_even, got_odd = exchange_both(y_even, y_odd, "sy")
    columns, x_even, x_odd = pl.pallas_call(
        functools.partial(update_kernel, h),
        out_shape=[own_type, column, column], in_specs=[SMEM] + [VMEM] * 8, out_specs=[VMEM] * 3, name="update",
    )(scale, y_even, y_odd, got_even, got_odd, object_re, object_im, up_even, up_odd)
    x_even, x_odd = exchange_both(x_even, x_odd, "sx")
    own, send_even, send_odd, keep, give = pl.pallas_call(
        functools.partial(later_batch_kernel, h, size, 1, True),
        out_shape=[own_type, column, column, f32(2, 2, f, h), f32(2, 2, f, h)],
        in_specs=[SMEM] * 2 + [VMEM] * 4 + fixed_specs, out_specs=[VMEM] * 5,
        scratch_shapes=batch_scratch(size, f, True), compiler_params=params, name="batch_last",
    )(visit_order, offsets, columns, x_even, x_odd, grads, *fixed_args)

    x_even, x_odd = exchange_both(send_even, send_odd, "sx")
    inner, y_even, y_odd = pl.pallas_call(
        functools.partial(fold_last_kernel, h),
        out_shape=[f32(2, 2, 2 * h, h), strip, strip], in_specs=[VMEM] * 3, out_specs=[VMEM] * 3, name="fold_last",
    )(own, x_even, x_odd)
    y_even, y_odd = exchange_both(y_even, y_odd, "sy")
    out_re, out_im = pl.pallas_call(
        functools.partial(finish_object_kernel, h),
        out_shape=[f32(2 * h, 2 * h)] * 2, in_specs=[SMEM] + [VMEM] * 4, out_specs=[VMEM] * 2, name="finish_object",
    )(scale, inner, y_even, y_odd, columns)

    groups = plan_groups()
    keep, give = keep.reshape(-1, h), give.reshape(-1, h)
    parts = [keep, group_exchange(give, groups[0], 1)]
    for group in groups[1:]:
        members = 1 << len(group)
        piece = f32(parts[0].shape[0] // members, h)
        pieces = pl.pallas_call(
            functools.partial(sum_kernel, group, len(parts)),
            out_shape=[piece] * members, in_specs=[VMEM] * len(parts), out_specs=[VMEM] * members, name="scatter_sum",
        )(*parts)
        parts = [pieces[0]] + [group_exchange(pieces[mask], group, mask) for mask in range(1, members)]
    total = sum(parts)
    for group in groups[:0:-1]:
        members = 1 << len(group)
        parts = [total] + [group_exchange(total, group, mask) for mask in range(1, members)]
        total = pl.pallas_call(
            functools.partial(gather_kernel, group),
            out_shape=f32(members * total.shape[0], h), in_specs=[VMEM] * members, out_specs=VMEM, name="gather",
        )(*parts)
    got = group_exchange(total, groups[0], 1)
    probe_rate = PROBE_GAIN / (positions * math.sqrt(lax.axis_size("sy") * lax.axis_size("sx")))
    piece = (2, 2, f, h)
    probe_out = pl.pallas_call(
        functools.partial(finish_probe_kernel, probe_rate),
        out_shape=[f32(2, f, f)] * 2, in_specs=[VMEM] * 4, out_specs=[VMEM] * 2, name="finish_probe",
    )(total.reshape(piece), got.reshape(piece), probe_re, probe_im)
    return (out_re, out_im, probe_out[0], probe_out[1])


def solution(mesh):
    return jax.shard_map(
        local,
        mesh=mesh,
        in_specs=(
            P("sy", "sx"),
            P("sy", "sx"),
            P(),
            P(),
            P("sy", "sx", None, None, None),
            P("sy", "sx", None, None),
            P("sy", "sx", None),
        ),
        out_specs=(P("sy", "sx"), P("sy", "sx"), P(), P()),
        check_vma=False,
    )
```

```python
import functools
import math

import jax
import jax.numpy as jnp
from jax import lax
from jax.experimental import pallas as pl
from jax.experimental.pallas import tpu as pltpu
from jax.sharding import PartitionSpec as P

BATCHES = 2
SY, SX = "sy", "sx"

OBJECT_RATE = 0.25
PROBE_GAIN = 4.0

VMEM = pl.BlockSpec(memory_space=pltpu.VMEM)
SMEM = pl.BlockSpec(memory_space=pltpu.SMEM)
HBM = pl.BlockSpec(memory_space=pltpu.HBM)


def call(kernel, out_shape, operands, in_specs=None, scratch=(), room=0):
    outs = jax.tree.leaves(out_shape)
    specs = in_specs or [VMEM] * len(operands)
    held = [a for a, spec in zip(operands, specs) if spec is VMEM]
    need = sum(a.dtype.itemsize * math.prod(a.shape) for a in held + outs) + room
    return pl.pallas_call(
        kernel,
        out_shape=out_shape,
        in_specs=specs,
        out_specs=jax.tree.map(lambda _: VMEM, out_shape),
        scratch_shapes=scratch,
        compiler_params=pltpu.CompilerParams(vmem_limit_bytes=need + (1 << 20)),
    )(*operands)


def f32(*shape):
    return jax.ShapeDtypeStruct(shape, jnp.float32)


def prepare_kernel(
    order, order_hbm, offs_hbm, re_hbm, im_hbm, amp_hbm,
    table_left, table_right, scale, order_out, offs, probe_re, probe_im, amp, sems,
):
    f = probe_re.shape[1]
    moves = [(order_hbm, order_out), (offs_hbm, offs), (re_hbm, probe_re), (im_hbm, probe_im)]
    moves += [(amp_hbm.at[0, 0, order[0, 0, j]], amp.at[j]) for j in range(amp.shape[0])]
    copies = [pltpu.make_async_copy(a, b, sems.at[i]) for i, (a, b) in enumerate(moves)]
    for copy in copies:
        copy.start()
    rows = lax.broadcasted_iota(jnp.int32, (f, f), 0)
    cols = lax.broadcasted_iota(jnp.int32, (f, f), 1)
    phase_angle = 2.0 * math.pi / f * lax.rem(rows * cols, f).astype(jnp.float32)
    norm_scale = 1.0 / math.sqrt(f)
    table_re = (jnp.cos(phase_angle) * norm_scale).astype(jnp.bfloat16)
    table_im = (-jnp.sin(phase_angle) * norm_scale).astype(jnp.bfloat16)
    for table, sign in ((table_left, 1), (table_right, -1)):
        table[:f, :f] = table_re
        table[f:, f:] = table_re
        table[:f, f:] = table_im if sign < 0 else -table_im
        table[f:, :f] = table_im if sign > 0 else -table_im
    for copy in copies:
        copy.wait()
    power = sum(part[m] * part[m] for part in (probe_re, probe_im) for m in range(2))
    scale[...] = OBJECT_RATE / jnp.broadcast_to(jnp.max(power), scale.shape)


def pair_exchange(block, axis, odd, bit=2):
    count_y, count_x = lax.axis_size(SY), lax.axis_size(SX)
    perm = []
    for y in range(count_y):
        for x in range(count_x):
            index, count = (y, count_y) if axis == SY else (x, count_x)
            partner = index + 1 if index % 2 == odd else index - 1
            if 0 <= partner < count:
                to_y, to_x = (partner, x) if axis == SY else (y, partner)
            else:
                to_y, to_x = (y, stand_in(x, count_x, bit)) if axis == SY else (stand_in(y, count_y, bit), x)
            perm.append((y * count_x + x, to_y * count_x + to_x))
    return lax.ppermute(block, (SY, SX), perm)


def stand_in(index, count, bit):
    other = index ^ bit
    return other if other < count else index


def has_partner(axis, odd):
    index, count = lax.axis_index(axis), lax.axis_size(axis)
    partner = jnp.where(lax.rem(index, 2) == odd, index + 1, index - 1)
    return (partner >= 0) & (partner < count)


def masked(axis, odd, block):
    return jnp.where(has_partner(axis, odd), block, 0.0)


def parity(axis):
    return lax.rem(lax.axis_index(axis), 2)


def aligned(value, unit):
    return pl.multiple_of(value, unit)


def pack_tile_kernel(h, obj_re, obj_im, *outs_and_sems):
    outs, sems = outs_and_sems[:-1], outs_and_sems[-1]
    y_even, y_odd, x_even, x_odd, tile = outs[:2], outs[2:4], outs[4], outs[5], outs[6]
    py, px = parity(SY), parity(SX)
    copies = []
    for c, obj in enumerate((obj_re, obj_im)):
        for out, side in ((y_even[c], 1 - py), (y_odd[c], py)):
            rows = pl.ds(aligned(side * h, h), h)
            copies += [(obj.at[rows, pl.ds(lb * h, h)], out.at[lb]) for lb in range(2)]
        for out, side in ((x_even, 1 - px), (x_odd, px)):
            copies.append((obj.at[:, pl.ds(aligned(side * h, h), h)], out.at[c]))
        copies += [(obj.at[:, pl.ds(lb * h, h)], tile.at[c, lb]) for lb in range(2)]
    copies = [pltpu.make_async_copy(a, b, sems.at[i]) for i, (a, b) in enumerate(copies)]
    for copy in copies:
        copy.start()
    for copy in copies:
        copy.wait()


def pack_corner_kernel(up_even, up_odd, c_even, c_odd):
    px = parity(SX)
    for odd, strip in enumerate((up_even, up_odd)):
        c_even[odd] = masked(SY, odd, strip[1 - px])
        c_odd[odd] = masked(SY, odd, strip[px])


def batch_body(
    batch, size, order, offs, probe, tables, amp, ext, accum, grads, grads_before, scratch
):
    sets = [scratch[i::2] for i in range(2)]
    f = probe[0].shape[1]
    h = f // 2
    rows = 16
    lane = lax.broadcasted_iota(jnp.int32, (rows, h), 1)
    table_left, table_right = tables

    def place(j):
        chosen = order[0, 0, batch * size + j]
        left = offs[0, 0, 1, chosen] + h
        return offs[0, 0, 0, chosen] + h, lax.div(left, h), lax.rem(left, h)

    def exits_of(j):
        patch, exits, *_ = sets[j % 2]
        top, first, shift = place(j)
        back_shift = lax.rem(h - shift, h)
        inside = lane < h - shift
        for r in range(0, f, rows):
            here = pl.ds(r, rows)
            window = []
            for c in range(2):
                a, b, d = [
                    pltpu.roll(ext[c, first + k, pl.ds(top + r, rows), :], back_shift, 1) for k in range(3)
                ]
                window.append([jnp.where(inside, a, b), jnp.where(inside, b, d)])
            for lb in range(2):
                o_re, o_im = window[0][lb], window[1][lb]
                patch[0, here, pl.ds(lb * h, h)] = o_re
                patch[1, here, pl.ds(lb * h, h)] = o_im
                for m in range(2):
                    p_re, p_im = [part[m, here, pl.ds(lb * h, h)] for part in probe]
                    spot = pl.ds(m * f + lb * h, h)
                    exits[pl.ds(r, rows), spot] = (p_re * o_re - p_im * o_im).astype(jnp.bfloat16)
                    exits[pl.ds(f + r, rows), spot] = (p_re * o_im + p_im * o_re).astype(jnp.bfloat16)

    def transform(j, values, first_table, second_table):
        mixed, field = sets[j % 2][3:]
        product = jnp.dot(first_table[...], values[...], preferred_element_type=jnp.float32)
        for c in range(2):
            for m in range(2):
                part = product[c * f : (c + 1) * f, m * f : (m + 1) * f]
                mixed[pl.ds(m * f, f), pl.ds(c * f, f)] = part.astype(jnp.bfloat16)
        field[...] = jnp.dot(mixed[...], second_table[...], preferred_element_type=jnp.float32)

    def forward(j):
        transform(j, sets[j % 2][1], table_left, table_right)

    def backward(j):
        transform(j, sets[j % 2][2], table_right, table_left)

    def correct(j):
        _, _, fixed, _, field = sets[j % 2]
        for r in range(0, f, rows):
            for lb in range(2):
                far = [
                    [field[pl.ds(m * f + r, rows), pl.ds(c * f + lb * h, h)] for c in range(2)] for m in range(2)
                ]
                power = sum(part * part for mode in far for part in mode)
                ratio = amp[j, pl.ds(r, rows), pl.ds(lb * h, h)] * lax.rsqrt(jnp.maximum(power, 1.0))
                for m in range(2):
                    for c in range(2):
                        spot = pl.ds(m * f + lb * h, h)
                        fixed[pl.ds(c * f + r, rows), spot] = (far[m][c] * ratio).astype(jnp.bfloat16)

    def gradients(j):
        patch, exits, _, _, field = sets[j % 2]
        top, first, shift = place(j)
        beyond = lane >= shift
        for r in range(0, f, rows):
            here = pl.ds(r, rows)
            term = [[0.0, 0.0], [0.0, 0.0]]
            for lb in range(2):
                cols = pl.ds(lb * h, h)
                o_re, o_im = patch[0, here, cols], patch[1, here, cols]
                for m in range(2):
                    d_re, d_im = [
                        field[pl.ds(m * f + r, rows), pl.ds(c * f + lb * h, h)]
                        - exits[pl.ds(c * f + r, rows), pl.ds(m * f + lb * h, h)].astype(jnp.float32)
                        for c in range(2)
                    ]
                    p_re, p_im = [part[m, here, cols] for part in probe]
                    term[0][lb] += p_re * d_re + p_im * d_im
                    term[1][lb] += p_re * d_im - p_im * d_re
                    for c, part in enumerate((o_re * d_re + o_im * d_im, o_re * d_im - o_im * d_re)):
                        sofar = grads if j else grads_before
                        grads[m, c, lb, here, :] = part if sofar is None else sofar[m, c, lb, here, :] + part
            for c in range(2):
                a, b = [pltpu.roll(part, shift, 1) for part in term[c]]
                there = pl.ds(top + r, rows)
                accum[c, first, there, :] += jnp.where(beyond, a, 0.0)
                accum[c, first + 1, there, :] += jnp.where(beyond, b, a)
                accum[c, first + 2, there, :] += jnp.where(beyond, 0.0, b)

    exits_of(0)
    for j in range(0, size, 2):
        pair = j + 1 < size
        forward(j)
        if j == 0:
            accum[...] = jnp.zeros_like(accum)
        else:
            gradients(j - 1)
        if pair:
            exits_of(j + 1)
            forward(j + 1)
        correct(j)
        backward(j)
        if pair:
            correct(j + 1)
            backward(j + 1)
        gradients(j)
        if j + 2 < size:
            exits_of(j + 2)
        elif pair:
            gradients(j + 1)


def first_batch_kernel(
    h, size, order, offs, tile, up_even_re, up_even_im, up_odd_re, up_odd_im, x_even, x_odd,
    c_even_re, c_even_im, c_odd_re, c_odd_im, probe_re, probe_im, table_left, table_right, amp, amp_hbm,
    ext, accum, send_even, send_00, send_01, send_10, send_11, grads, amp_next, amp_sems, *scratch,
):
    py, px = parity(SY), parity(SX)
    copies = [
        pltpu.make_async_copy(amp_hbm.at[0, 0, order[0, 0, size + j]], amp_next.at[j], amp_sems.at[j]) for j in range(size)
    ]
    for copy in copies:
        copy.start()
    halo_rows = [pl.ds(aligned(side * 3 * h, h), h) for side in (1 - py, py)]
    ups = ((up_even_re, up_odd_re), (up_even_im, up_odd_im))
    corners = ((c_even_re, c_odd_re), (c_even_im, c_odd_im))
    for c in range(2):
        for lb in range(2):
            ext[c, 1 + lb, h : 3 * h] = tile[c, lb]
            for odd in range(2):
                ext[c, 1 + lb, halo_rows[odd]] = masked(SY, odd, ups[c][odd][lb])
        for odd, (block, column) in enumerate((((1 - px) * 3, x_even), (px * 3, x_odd))):
            ext[c, block, h : 3 * h] = masked(SX, odd, column[c])
            for odd_row in range(2):
                ext[c, block, halo_rows[odd_row]] = masked(SX, odd, corners[c][odd][odd_row])
    probe, tables = (probe_re, probe_im), (table_left, table_right)
    batch_body(0, size, order, offs, probe, tables, amp, ext, accum, grads, None, scratch)
    for copy in copies:
        copy.wait()
    for c, sends in enumerate(((send_00, send_01), (send_10, send_11))):
        send_even[c] = accum[c, (1 - px) * 3]
        for odd, send in enumerate(sends):
            send[...] = accum[c, px * 3, half_rows(h, odd)]


def last_batch_kernel(
    h, size, batch, order, offs, columns_00, columns_01, columns_10, columns_11, x_even, odd_00, odd_01, odd_10, odd_11,
    grads_in, probe_re, probe_im, table_left, table_right, amp, accum, send_even, send_odd, keep, give, ext, grads, *scratch,
):
    px = parity(SX)
    columns = ((columns_00, columns_01), (columns_10, columns_11))
    x_odd = ((odd_00, odd_01), (odd_10, odd_11))
    for c in range(2):
        for odd in range(2):
            rows = half_rows(h, odd)
            for lb in range(2):
                ext[c, 1 + lb, rows] = columns[c][odd][lb]
            ext[c, (1 - px) * 3, rows] = masked(SX, 0, x_even[c, odd])
            ext[c, px * 3, rows] = masked(SX, 1, x_odd[c][odd][...])
    probe, tables = (probe_re, probe_im), (table_left, table_right)
    batch_body(batch, size, order, offs, probe, tables, amp, ext, accum, grads, grads_in, scratch)
    keep[...] = grads[px]
    give[...] = grads[1 - px]
    for c in range(2):
        send_even[c] = accum[c, (1 - px) * 3]
        send_odd[c] = accum[c, px * 3]


def batch_scratch(f):
    flat = [pltpu.VMEM((2 * f, 2 * f), dtype) for dtype in (jnp.bfloat16,) * 3 + (jnp.float32,)]
    each = [pltpu.VMEM((2, f, f), jnp.float32), *flat]
    return [buffer for buffer in each for _ in range(2)]


def half_side(odd):
    py = parity(SY)
    return py if odd else 1 - py


def half_rows(h, odd):
    return pl.ds(aligned(half_side(odd) * 2 * h, 2 * h), 2 * h)


def fold_columns_kernel(h, c, odd, accum, x_even, x_odd, y_send):
    px = parity(SX)
    rows = half_rows(h, odd)
    columns = masked(SX, 0, x_even[c, rows]), masked(SX, 1, x_odd[...])
    for block, column in zip((1 - px, px), columns):
        y_send[block] = accum[c, 1 + block, rows] + column


def update_kernel(h, c, odd, scale, y_send, y_got, ext, columns, x_send):
    px, side = parity(SX), half_side(odd)
    rate = scale[0:1, :]
    rate_halo = jnp.where(has_partner(SY, odd), rate, 0.0)
    for lb in range(2):
        for at, factor in ((1 - side, rate), (side, rate_halo)):
            here = pl.ds(aligned(at * h, h), h)
            there = pl.ds(aligned((2 * side + at) * h, h), h)
            total = y_send[lb, here] + masked(SY, odd, y_got[lb, here])
            columns[lb, here] = ext[c, 1 + lb, there] + factor * total
    x_send[...] = columns[px]


def pack_even_kernel(columns_00, columns_01, columns_10, columns_11, x_even):
    px = parity(SX)
    for c, parts in enumerate(((columns_00, columns_01), (columns_10, columns_11))):
        for odd, part in enumerate(parts):
            x_even[c, odd] = part[1 - px]


def fold_last_kernel(h, accum, x_even, x_odd, inner, y_even, y_odd):
    py, px = parity(SY), parity(SX)
    for c in range(2):
        columns = masked(SX, 0, x_even[c]), masked(SX, 1, x_odd[c])
        for block, column in zip((1 - px, px), columns):
            total = accum[c, 1 + block] + column
            inner[c, block] = total[h : 3 * h]
            y_even[c, block] = jnp.where(py == 0, total[3 * h :], total[:h])
            y_odd[c, block] = jnp.where(py == 0, total[:h], total[3 * h :])


def finish_object_kernel(
    h, scale, inner, y_even, y_odd, columns_00, columns_01, columns_10, columns_11, out_re, out_im
):
    rate = scale[0:1, :]
    columns = ((columns_00, columns_01), (columns_10, columns_11))
    for c, out in enumerate((out_re, out_im)):
        for lb in range(2):
            for odd, got in enumerate((y_even, y_odd)):
                side = half_side(odd)
                here = pl.ds(aligned(side * h, h), h)
                old = columns[c][odd][lb, pl.ds(aligned((1 - side) * h, h), h)]
                total = inner[c, lb, here] + masked(SY, odd, got[c, lb])
                out[here, lb * h : (lb + 1) * h] = old + rate * total


def plan_bits():
    bits = {axis: lax.axis_size(axis).bit_length() - 1 for axis in (SY, SX)}
    for axis, count in bits.items():
        if 1 << count != lax.axis_size(axis):
            raise ValueError("axis size")
    first, *across = [(SX, bit) for bit in range(bits[SX])]
    along = [(SY, bit) for bit in range(bits[SY])]
    block = along[:2] + across[:1]
    return first, block, along[2:] + across[1:]


def flip_exchange(block, axis, bit):
    count_y, count_x = lax.axis_size(SY), lax.axis_size(SX)
    flip_y, flip_x = (1 << bit, 0) if axis == SY else (0, 1 << bit)
    perm = [(y * count_x + x, (y ^ flip_y) * count_x + (x ^ flip_x)) for y in range(count_y) for x in range(count_x)]
    return lax.ppermute(block, (SY, SX), perm)


def block_exchange(pieces, bits):
    count_y, count_x = lax.axis_size(SY), lax.axis_size(SX)
    mask_y, mask_x = [sum(1 << bit for axis, bit in bits if axis == own) for own in (SY, SX)]
    groups = {}
    for y in range(count_y):
        for x in range(count_x):
            groups.setdefault((y & ~mask_y, x & ~mask_x), []).append(y * count_x + x)
    return lax.all_to_all(pieces, (SY, SX), 0, 0, tiled=True, axis_index_groups=list(groups.values()))


def sum_kernel(left, right, out):
    out[...] = left[...] + right[...]


def sum_block_kernel(pieces, out):
    size = out.shape[0]
    out[...] = sum(pieces[at : at + size, :] for at in range(0, pieces.shape[0], size))


def spread_kernel(left, right, out):
    total = left[...] + right[...]
    size = total.shape[0]
    for at in range(0, out.shape[0], size):
        out[at : at + size, :] = total


def finish_probe_kernel(rate, keep, got, probe_re, probe_im, out_re, out_im):
    px = parity(SX)
    f = probe_re.shape[1]
    h = f // 2
    for mode, part in ((px, keep), (1 - px, got)):
        for c, (probe, out) in enumerate(((probe_re, out_re), (probe_im, out_im))):
            for lb in range(2):
                cols = slice(lb * h, (lb + 1) * h)
                out[mode, :, cols] = probe[mode, :, cols] + rate * part[c, lb]


def local(object_re, object_im, probe_re, probe_im, amplitudes, offsets, visit_order):
    f = probe_re.shape[1]
    h = f // 2
    positions = visit_order.shape[-1]
    size = positions // BATCHES
    table_type = jax.ShapeDtypeStruct((2 * f, 2 * f), jnp.bfloat16)
    in_hbm = functools.partial(pltpu.with_memory_space_constraint, memory_space=pltpu.HBM)
    offsets = offsets.transpose(0, 1, 3, 2)
    arrays = (visit_order, offsets, probe_re, probe_im)
    table_left, table_right, scale, *arrays, amp = call(
        prepare_kernel,
        [table_type, table_type, f32(8, h)] + [jax.ShapeDtypeStruct(a.shape, a.dtype) for a in arrays] + [f32(size, f, f)],
        (visit_order, *map(in_hbm, arrays), in_hbm(amplitudes)),
        [SMEM] + [HBM] * 5,
        [pltpu.SemaphoreType.DMA((4 + size,))],
    )
    visit_order, offsets, *probe = arrays
    strip = f32(2, h, h)
    block = f32(2, 2 * h, h)
    up = call(
        functools.partial(pack_tile_kernel, h),
        [strip] * 4 + [block] * 2 + [f32(2, 2, 2 * h, h)],
        (in_hbm(object_re), in_hbm(object_im)),
        [HBM] * 2,
        [pltpu.SemaphoreType.DMA((16,))],
    )
    up_even = [pair_exchange(up[c], SY, 0) for c in range(2)]
    up_odd = [pair_exchange(up[2 + c], SY, 1) for c in range(2)]
    x_even = pair_exchange(up[4], SX, 0)
    x_odd = pair_exchange(up[5], SX, 1)
    corners = [call(pack_corner_kernel, [strip, strip], (up_even[c], up_odd[c])) for c in range(2)]
    c_even = [pair_exchange(corners[c][0], SX, 0) for c in range(2)]
    c_odd = [pair_exchange(corners[c][1], SX, 1) for c in range(2)]

    column, columns_type = f32(2 * h, h), f32(2, 4 * h, h)
    ext_type, grads_type = f32(2, 4, 4 * h, h), f32(2, 2, 2, f, h)
    fixed_args = (*probe, table_left, table_right)
    fixed_specs = [VMEM] * 4
    ext, accum, send_even, *send_odd, grads, amp_next = call(
        functools.partial(first_batch_kernel, h, size),
        [ext_type, ext_type, columns_type] + [column] * 4 + [grads_type, f32(size, f, f)],
        (visit_order, offsets, up[6], *up_even, *up_odd, x_even, x_odd, *c_even, *c_odd, *fixed_args, amp, in_hbm(amplitudes)),
        [SMEM] * 2 + [VMEM] * 12 + fixed_specs + [HBM],
        [pltpu.SemaphoreType.DMA((size,)), *batch_scratch(f)],
        9 << 20,
    )

    streams = [(c, odd) for c in range(2) for odd in range(2)]
    x_even = pair_exchange(send_even, SX, 0)
    columns, x_odd = [], []
    for (c, odd), part in zip(streams, send_odd):
        x_got = pair_exchange(part, SX, 1)
        y_send = call(functools.partial(fold_columns_kernel, h, c, odd), block, (accum, x_even, x_got))
        y_got = pair_exchange(y_send, SY, odd)
        new, x_send = call(functools.partial(update_kernel, h, c, odd), [block, column], (scale, y_send, y_got, ext))
        columns.append(new)
        x_odd.append(pair_exchange(x_send, SX, 1))
    x_send = call(pack_even_kernel, f32(2, 2, 2 * h, h), columns)
    x_even = pair_exchange(x_send, SX, 0)
    modes = f32(2, 2, f, h)
    accum, send_even, send_odd, keep, give = call(
        functools.partial(last_batch_kernel, h, size, 1),
        [ext_type, columns_type, columns_type, modes, modes],
        (visit_order, offsets, *columns, x_even, *x_odd, grads, *fixed_args, amp_next),
        [SMEM] * 2 + [VMEM] * 11 + fixed_specs,
        [pltpu.VMEM(t.shape, t.dtype) for t in (ext_type, grads_type)] + batch_scratch(f),
        12 << 20,
    )

    x_odd = pair_exchange(send_odd, SX, 1, 1)
    x_even = pair_exchange(send_even, SX, 0)
    last = f32(2, 2, h, h)
    inner, y_even, y_odd = call(
        functools.partial(fold_last_kernel, h), [f32(2, 2, 2 * h, h), last, last], (accum, x_even, x_odd)
    )
    y_even = pair_exchange(y_even, SY, 0)
    y_odd = pair_exchange(y_odd, SY, 1)
    out_re, out_im = call(
        functools.partial(finish_object_kernel, h), [f32(2 * h, 2 * h)] * 2, (scale, inner, y_even, y_odd, *columns)
    )

    first, block_bits, pairs = plan_bits()
    keep, give = keep.reshape(-1, h), give.reshape(-1, h)
    both = call(sum_kernel, f32(*keep.shape), (keep, flip_exchange(give, *first)))
    pieces = block_exchange(both, block_bits)
    total = call(sum_block_kernel, f32(keep.shape[0] >> len(block_bits), h), (pieces,))
    for at, (axis, bit) in enumerate(pairs):
        got = flip_exchange(total, axis, bit)
        last_pair = at == len(pairs) - 1
        kernel, shape = (spread_kernel, keep.shape) if last_pair else (sum_kernel, total.shape)
        total = call(kernel, f32(*shape), (total, got))
    total = block_exchange(total, block_bits)
    got = flip_exchange(total, *first)
    probe_rate = PROBE_GAIN / (positions * math.sqrt(lax.axis_size(SY) * lax.axis_size(SX)))
    piece = (2, 2, f, h)
    probe_out = call(
        functools.partial(finish_probe_kernel, probe_rate),
        [f32(2, f, f)] * 2,
        (total.reshape(piece), got.reshape(piece), *probe),
    )
    return (out_re, out_im, probe_out[0], probe_out[1])


def solution(mesh):
    return jax.shard_map(
        local,
        mesh=mesh,
        in_specs=(
            P(SY, SX),
            P(SY, SX),
            P(),
            P(),
            P(SY, SX, None, None, None),
            P(SY, SX, None, None),
            P(SY, SX, None),
        ),
        out_specs=(P(SY, SX), P(SY, SX), P(), P()),
        check_vma=False,
    )
```

```python
import functools
import math

import jax
import jax.numpy as jnp
from jax import lax
from jax.experimental import pallas as pl
from jax.experimental.pallas import tpu as pltpu
from jax.sharding import PartitionSpec as P

BATCHES = 2
SY, SX = "sy", "sx"

OBJECT_RATE = 0.25
PROBE_GAIN = 4.0

VMEM = pl.BlockSpec(memory_space=pltpu.VMEM)
SMEM = pl.BlockSpec(memory_space=pltpu.SMEM)
HBM = pl.BlockSpec(memory_space=pltpu.HBM)


def call(kernel, out_shape, operands, in_specs=None, scratch=(), room=0):
    outs = jax.tree.leaves(out_shape)
    specs = in_specs or [VMEM] * len(operands)
    held = [a for a, spec in zip(operands, specs) if spec is VMEM]
    need = sum(a.dtype.itemsize * math.prod(a.shape) for a in held + outs) + room
    return pl.pallas_call(
        kernel,
        out_shape=out_shape,
        in_specs=specs,
        out_specs=jax.tree.map(lambda _: VMEM, out_shape),
        scratch_shapes=scratch,
        compiler_params=pltpu.CompilerParams(vmem_limit_bytes=need + (1 << 20)),
    )(*operands)


def f32(*shape):
    return jax.ShapeDtypeStruct(shape, jnp.float32)


def prepare_kernel(
    order, order_hbm, offs_hbm, re_hbm, im_hbm, amp_hbm,
    table_left, table_right, scale, order_out, offs, probe_re, probe_im, amp, sems,
):
    f = probe_re.shape[1]
    moves = [(order_hbm, order_out), (offs_hbm, offs), (re_hbm, probe_re), (im_hbm, probe_im)]
    moves += [(amp_hbm.at[0, 0, order[0, 0, j]], amp.at[j]) for j in range(amp.shape[0])]
    copies = [pltpu.make_async_copy(a, b, sems.at[i]) for i, (a, b) in enumerate(moves)]
    for copy in copies:
        copy.start()
    rows = lax.broadcasted_iota(jnp.int32, (f, f), 0)
    cols = lax.broadcasted_iota(jnp.int32, (f, f), 1)
    phase_angle = 2.0 * math.pi / f * lax.rem(rows * cols, f).astype(jnp.float32)
    norm_scale = 1.0 / math.sqrt(f)
    table_re = (jnp.cos(phase_angle) * norm_scale).astype(jnp.bfloat16)
    table_im = (-jnp.sin(phase_angle) * norm_scale).astype(jnp.bfloat16)
    for table, sign in ((table_left, 1), (table_right, -1)):
        table[:f, :f] = table_re
        table[f:, f:] = table_re
        table[:f, f:] = table_im if sign < 0 else -table_im
        table[f:, :f] = table_im if sign > 0 else -table_im
    for copy in copies:
        copy.wait()
    power = sum(part[m] * part[m] for part in (probe_re, probe_im) for m in range(2))
    scale[...] = OBJECT_RATE / jnp.broadcast_to(jnp.max(power), scale.shape)


def pair_exchange(block, axis, odd, bit=2):
    count_y, count_x = lax.axis_size(SY), lax.axis_size(SX)
    perm = []
    for y in range(count_y):
        for x in range(count_x):
            index, count = (y, count_y) if axis == SY else (x, count_x)
            partner = index + 1 if index % 2 == odd else index - 1
            if 0 <= partner < count:
                to_y, to_x = (partner, x) if axis == SY else (y, partner)
            else:
                to_y, to_x = (y, stand_in(x, count_x, bit)) if axis == SY else (stand_in(y, count_y, bit), x)
            perm.append((y * count_x + x, to_y * count_x + to_x))
    return lax.ppermute(block, (SY, SX), perm)


def stand_in(index, count, bit):
    other = index ^ bit
    return other if other < count else index


def has_partner(axis, odd):
    index, count = lax.axis_index(axis), lax.axis_size(axis)
    partner = jnp.where(lax.rem(index, 2) == odd, index + 1, index - 1)
    return (partner >= 0) & (partner < count)


def masked(axis, odd, block):
    return jnp.where(has_partner(axis, odd), block, 0.0)


def parity(axis):
    return lax.rem(lax.axis_index(axis), 2)


def aligned(value, unit):
    return pl.multiple_of(value, unit)


def run_copies(pairs, sems):
    copies = [pltpu.make_async_copy(a, b, sems.at[i]) for i, (a, b) in enumerate(pairs)]
    for copy in copies:
        copy.start()
    for copy in copies:
        copy.wait()


def lane_block(far):
    px = parity(SX)
    return px if far else 1 - px


def pack_rows_kernel(h, obj_re, obj_im, *outs_and_sems):
    *outs, sems = outs_and_sems
    py = parity(SY)
    pairs = []
    for at, out in enumerate(outs):
        far, odd = divmod(at, 2)
        rows = pl.ds(aligned((py if odd else 1 - py) * h, h), h)
        columns = pl.ds(aligned(lane_block(far) * h, h), h)
        pairs += [(obj.at[rows, columns], out.at[c]) for c, obj in enumerate((obj_re, obj_im))]
    run_copies(pairs, sems)


def pack_columns_kernel(h, obj_re, obj_im, x_even, x_odd, tile, sems):
    px = parity(SX)
    pairs = []
    for c, obj in enumerate((obj_re, obj_im)):
        for out, side in ((x_even, 1 - px), (x_odd, px)):
            pairs.append((obj.at[:, pl.ds(aligned(side * h, h), h)], out.at[c]))
        pairs += [(obj.at[:, pl.ds(lb * h, h)], tile.at[c, lb]) for lb in range(2)]
    run_copies(pairs, sems)


def pack_corner_kernel(up_even, up_odd, corner):
    for odd, strip in enumerate((up_even, up_odd)):
        corner[odd] = masked(SY, odd, strip[...])


def batch_body(
    batch, size, order, offs, probe, tables, amp, ext, accum, grads, grads_before, scratch
):
    sets = [scratch[i::2] for i in range(2)]
    f = probe[0].shape[1]
    h = f // 2
    rows = 16
    lane = lax.broadcasted_iota(jnp.int32, (rows, h), 1)
    table_left, table_right = tables

    def place(j):
        chosen = order[0, 0, batch * size + j]
        left = offs[0, 0, 1, chosen] + h
        return offs[0, 0, 0, chosen] + h, lax.div(left, h), lax.rem(left, h)

    def exits_of(j):
        patch, exits, *_ = sets[j % 2]
        top, first, shift = place(j)
        back_shift = lax.rem(h - shift, h)
        inside = lane < h - shift
        for r in range(0, f, rows):
            here = pl.ds(r, rows)
            window = []
            for c in range(2):
                a, b, d = [
                    pltpu.roll(ext[c, first + k, pl.ds(top + r, rows), :], back_shift, 1) for k in range(3)
                ]
                window.append([jnp.where(inside, a, b), jnp.where(inside, b, d)])
            for lb in range(2):
                o_re, o_im = window[0][lb], window[1][lb]
                patch[0, here, pl.ds(lb * h, h)] = o_re
                patch[1, here, pl.ds(lb * h, h)] = o_im
                for m in range(2):
                    p_re, p_im = [part[m, here, pl.ds(lb * h, h)] for part in probe]
                    spot = pl.ds(m * f + lb * h, h)
                    exits[pl.ds(r, rows), spot] = (p_re * o_re - p_im * o_im).astype(jnp.bfloat16)
                    exits[pl.ds(f + r, rows), spot] = (p_re * o_im + p_im * o_re).astype(jnp.bfloat16)

    def transform(j, values, first_table, second_table):
        mixed, field = sets[j % 2][3:]
        product = jnp.dot(first_table[...], values[...], preferred_element_type=jnp.float32)
        for c in range(2):
            for m in range(2):
                part = product[c * f : (c + 1) * f, m * f : (m + 1) * f]
                mixed[pl.ds(m * f, f), pl.ds(c * f, f)] = part.astype(jnp.bfloat16)
        field[...] = jnp.dot(mixed[...], second_table[...], preferred_element_type=jnp.float32)

    def forward(j):
        transform(j, sets[j % 2][1], table_left, table_right)

    def backward(j):
        transform(j, sets[j % 2][2], table_right, table_left)

    def correct(j):
        _, _, fixed, _, field = sets[j % 2]
        for r in range(0, f, rows):
            for lb in range(2):
                far = [
                    [field[pl.ds(m * f + r, rows), pl.ds(c * f + lb * h, h)] for c in range(2)] for m in range(2)
                ]
                power = sum(part * part for mode in far for part in mode)
                ratio = amp[batch * size + j, pl.ds(r, rows), pl.ds(lb * h, h)] * lax.rsqrt(jnp.maximum(power, 1.0))
                for m in range(2):
                    for c in range(2):
                        spot = pl.ds(m * f + lb * h, h)
                        fixed[pl.ds(c * f + r, rows), spot] = (far[m][c] * ratio).astype(jnp.bfloat16)

    def gradients(j):
        patch, exits, _, _, field = sets[j % 2]
        top, first, shift = place(j)
        beyond = lane >= shift
        for r in range(0, f, rows):
            here = pl.ds(r, rows)
            term = [[0.0, 0.0], [0.0, 0.0]]
            for lb in range(2):
                cols = pl.ds(lb * h, h)
                o_re, o_im = patch[0, here, cols], patch[1, here, cols]
                for m in range(2):
                    d_re, d_im = [
                        field[pl.ds(m * f + r, rows), pl.ds(c * f + lb * h, h)]
                        - exits[pl.ds(c * f + r, rows), pl.ds(m * f + lb * h, h)].astype(jnp.float32)
                        for c in range(2)
                    ]
                    p_re, p_im = [part[m, here, cols] for part in probe]
                    term[0][lb] += p_re * d_re + p_im * d_im
                    term[1][lb] += p_re * d_im - p_im * d_re
                    for c, part in enumerate((o_re * d_re + o_im * d_im, o_re * d_im - o_im * d_re)):
                        sofar = grads if j else grads_before
                        grads[m, c, lb, here, :] = part if sofar is None else sofar[m, c, lb, here, :] + part
            for c in range(2):
                a, b = [pltpu.roll(part, shift, 1) for part in term[c]]
                there = pl.ds(top + r, rows)
                accum[c, first, there, :] += jnp.where(beyond, a, 0.0)
                accum[c, first + 1, there, :] += jnp.where(beyond, b, a)
                accum[c, first + 2, there, :] += jnp.where(beyond, 0.0, b)

    exits_of(0)
    for j in range(0, size, 2):
        pair = j + 1 < size
        forward(j)
        if j == 0:
            accum[...] = jnp.zeros_like(accum)
        else:
            gradients(j - 1)
        if pair:
            exits_of(j + 1)
            forward(j + 1)
        correct(j)
        backward(j)
        if pair:
            correct(j + 1)
            backward(j + 1)
        gradients(j)
        if j + 2 < size:
            exits_of(j + 2)
        elif pair:
            gradients(j + 1)


def first_batch_kernel(
    h, size, order, offs, tile, up_00, up_01, up_10, up_11, x_even, x_odd, c_even, c_odd,
    probe_re, probe_im, table_left, table_right, amp,
    ext, accum, send_even, send_odd_re, send_odd_im, grads, *scratch,
):
    py, px = parity(SY), parity(SX)
    halo_rows = [pl.ds(aligned(side * 3 * h, h), h) for side in (1 - py, py)]
    ups = ((up_00, up_01), (up_10, up_11))
    for c in range(2):
        for lb in range(2):
            ext[c, 1 + lb, h : 3 * h] = tile[c, lb]
        for far, (block, column, corner) in enumerate((((1 - px) * 3, x_even, c_even), (px * 3, x_odd, c_odd))):
            ext[c, block, h : 3 * h] = masked(SX, far, column[c])
            for odd in range(2):
                ext[c, 1 + lane_block(far), halo_rows[odd]] = masked(SY, odd, ups[far][odd][c])
                ext[c, block, halo_rows[odd]] = masked(SX, far, corner[odd, c])
    probe, tables = (probe_re, probe_im), (table_left, table_right)
    batch_body(0, size, order, offs, probe, tables, amp, ext, accum, grads, None, scratch)
    for c, send_odd in enumerate((send_odd_re, send_odd_im)):
        send_even[c] = accum[c, (1 - px) * 3]
        send_odd[...] = accum[c, px * 3]


def last_batch_kernel(
    size, batch, order, offs, near_re, near_im, far_re, far_im, even_re, even_im, odd_re, odd_im, grads_in,
    probe_re, probe_im, table_left, table_right, amp, accum, send_even, send_odd, keep, give, ext, grads, *scratch,
):
    px = parity(SX)
    for c, parts in enumerate(((near_re, far_re, even_re, odd_re), (near_im, far_im, even_im, odd_im))):
        near, far, x_even, x_odd = parts
        ext[c, 1 + lane_block(0)] = near[...]
        ext[c, 1 + lane_block(1)] = far[...]
        ext[c, (1 - px) * 3] = masked(SX, 0, x_even[...])
        ext[c, px * 3] = masked(SX, 1, x_odd[...])
    probe, tables = (probe_re, probe_im), (table_left, table_right)
    batch_body(batch, size, order, offs, probe, tables, amp, ext, accum, grads, grads_in, scratch)
    keep[...] = grads[px]
    give[...] = grads[1 - px]
    for c in range(2):
        send_even[c] = accum[c, (1 - px) * 3]
        send_odd[c] = accum[c, px * 3]


def batch_scratch(f):
    flat = [pltpu.VMEM((2 * f, 2 * f), dtype) for dtype in (jnp.bfloat16,) * 3 + (jnp.float32,)]
    each = [pltpu.VMEM((2, f, f), jnp.float32), *flat]
    return [buffer for buffer in each for _ in range(2)]


def half_side(odd):
    py = parity(SY)
    return py if odd else 1 - py


def half_rows(h, odd):
    return pl.ds(aligned(half_side(odd) * 2 * h, 2 * h), 2 * h)


def fold_columns_kernel(h, c, far, accum, x_got, y_even, y_odd):
    for odd, y_send in enumerate((y_even, y_odd)):
        rows = half_rows(h, odd)
        column = x_got[rows] if far else x_got[c, rows]
        y_send[...] = accum[c, 1 + lane_block(far), rows] + masked(SX, far, column)


def update_kernel(h, c, far, scale, sent_even, got_even, sent_odd, got_odd, ext, columns):
    rate = scale[0:1, :]
    for odd, sent, got in ((0, sent_even, got_even), (1, sent_odd, got_odd)):
        side = half_side(odd)
        rate_halo = jnp.where(has_partner(SY, odd), rate, 0.0)
        for at, factor in ((1 - side, rate), (side, rate_halo)):
            here = pl.ds(aligned(at * h, h), h)
            there = pl.ds(aligned((2 * side + at) * h, h), h)
            total = sent[here] + masked(SY, odd, got[here])
            columns[there] = ext[c, 1 + lane_block(far), there] + factor * total


def fold_last_kernel(h, accum, x_even, x_odd, inner, y_even, y_odd):
    py = parity(SY)
    for far, x_got in enumerate((x_even, x_odd)):
        for c in range(2):
            total = accum[c, 1 + lane_block(far)] + masked(SX, far, x_got[c])
            inner[far, c] = total[h : 3 * h]
            y_even[far, c] = jnp.where(py == 0, total[3 * h :], total[:h])
            y_odd[far, c] = jnp.where(py == 0, total[:h], total[3 * h :])


def finish_object_kernel(h, scale, inner, y_even, y_odd, near_re, near_im, far_re, far_im, *outs):
    columns = (near_re, near_im), (far_re, far_im)
    rate = scale[0:1, :]
    for far in range(2):
        lanes = pl.ds(aligned(lane_block(far) * h, h), h)
        for c, out in enumerate(outs):
            for odd, got in enumerate((y_even, y_odd)):
                side = half_side(odd)
                here = pl.ds(aligned(side * h, h), h)
                old = columns[far][c][pl.ds(aligned((1 + side) * h, h), h)]
                out[here, lanes] = old + rate * (inner[far, c, here] + masked(SY, odd, got[far, c]))


def plan_bits():
    bits = {axis: lax.axis_size(axis).bit_length() - 1 for axis in (SY, SX)}
    for axis, count in bits.items():
        if 1 << count != lax.axis_size(axis):
            raise ValueError("axis size")
    first, *across = [(SX, bit) for bit in range(bits[SX])]
    along = [(SY, bit) for bit in range(bits[SY])]
    block = along[:2] + across[:1]
    return first, block, along[2:] + across[1:]


def flip_exchange(block, axis, bit):
    count_y, count_x = lax.axis_size(SY), lax.axis_size(SX)
    flip_y, flip_x = (1 << bit, 0) if axis == SY else (0, 1 << bit)
    perm = [(y * count_x + x, (y ^ flip_y) * count_x + (x ^ flip_x)) for y in range(count_y) for x in range(count_x)]
    return lax.ppermute(block, (SY, SX), perm)


def block_exchange(pieces, bits):
    count_y, count_x = lax.axis_size(SY), lax.axis_size(SX)
    mask_y, mask_x = [sum(1 << bit for axis, bit in bits if axis == own) for own in (SY, SX)]
    groups = {}
    for y in range(count_y):
        for x in range(count_x):
            groups.setdefault((y & ~mask_y, x & ~mask_x), []).append(y * count_x + x)
    return lax.all_to_all(pieces, (SY, SX), 0, 0, tiled=True, axis_index_groups=list(groups.values()))


def sum_kernel(left, right, out):
    out[...] = left[...] + right[...]


def sum_block_kernel(pieces, out):
    size = out.shape[0]
    out[...] = sum(pieces[at : at + size, :] for at in range(0, pieces.shape[0], size))


def spread_kernel(left, right, out):
    total = left[...] + right[...]
    size = total.shape[0]
    for at in range(0, out.shape[0], size):
        out[at : at + size, :] = total


def finish_probe_kernel(rate, keep, got, probe_re, probe_im, out_re, out_im):
    px = parity(SX)
    f = probe_re.shape[1]
    h = f // 2
    for mode, part in ((px, keep), (1 - px, got)):
        for c, (probe, out) in enumerate(((probe_re, out_re), (probe_im, out_im))):
            for lb in range(2):
                cols = slice(lb * h, (lb + 1) * h)
                out[mode, :, cols] = probe[mode, :, cols] + rate * part[c, lb]


def local(object_re, object_im, probe_re, probe_im, amplitudes, offsets, visit_order):
    f = probe_re.shape[1]
    h = f // 2
    positions = visit_order.shape[-1]
    size = positions // BATCHES
    table_type = jax.ShapeDtypeStruct((2 * f, 2 * f), jnp.bfloat16)
    in_hbm = functools.partial(pltpu.with_memory_space_constraint, memory_space=pltpu.HBM)
    offsets = offsets.transpose(0, 1, 3, 2)
    arrays = (visit_order, offsets, probe_re, probe_im)
    table_left, table_right, scale, *arrays, amp = call(
        prepare_kernel,
        [table_type, table_type, f32(8, h)] + [jax.ShapeDtypeStruct(a.shape, a.dtype) for a in arrays] + [f32(positions, f, f)],
        (visit_order, *map(in_hbm, arrays), in_hbm(amplitudes)),
        [SMEM] + [HBM] * 5,
        [pltpu.SemaphoreType.DMA((4 + positions,))],
    )
    visit_order, offsets, *probe = arrays
    strip = f32(2, h, h)
    block = f32(2, 2 * h, h)
    objects = in_hbm(object_re), in_hbm(object_im)
    sems = [pltpu.SemaphoreType.DMA((8,))]
    up = call(functools.partial(pack_rows_kernel, h), [strip] * 4, objects, [HBM] * 2, sems)
    x_even, x_odd, tile = call(
        functools.partial(pack_columns_kernel, h), [block, block, f32(2, 2, 2 * h, h)], objects, [HBM] * 2, sems
    )
    ups = {}
    for far in (1, 0):
        ups[far] = [pair_exchange(up[2 * far + odd], SY, odd) for odd in range(2)]
    x_even = pair_exchange(x_even, SX, 0)
    x_odd = pair_exchange(x_odd, SX, 1)
    corners = [pair_exchange(call(pack_corner_kernel, f32(2, 2, h, h), ups[far]), SX, far) for far in range(2)]

    column, columns_type = f32(4 * h, h), f32(2, 4 * h, h)
    ext_type, grads_type = f32(2, 4, 4 * h, h), f32(2, 2, 2, f, h)
    fixed_args = (*probe, table_left, table_right)
    fixed_specs = [VMEM] * 4
    ext, accum, send_even, *send_odd, grads = call(
        functools.partial(first_batch_kernel, h, size),
        [ext_type, ext_type, columns_type, column, column, grads_type],
        (visit_order, offsets, tile, *ups[0], *ups[1], x_even, x_odd, *corners, *fixed_args, amp),
        [SMEM] * 2 + [VMEM] * 10 + fixed_specs,
        batch_scratch(f),
        9 << 20,
    )

    half = f32(2 * h, h)
    x_even = pair_exchange(send_even, SX, 0)
    x_odd = [pair_exchange(part, SX, 1) for part in send_odd]
    columns, halos = {}, {}
    for far, c in ((0, 0), (1, 0), (1, 1), (0, 1)):
        sent = call(
            functools.partial(fold_columns_kernel, h, c, far), [half, half], (accum, x_odd[c] if far else x_even)
        )
        got = [pair_exchange(part, SY, odd) for odd, part in enumerate(sent)]
        columns[far, c] = call(
            functools.partial(update_kernel, h, c, far), column, (scale, sent[0], got[0], sent[1], got[1], ext)
        )
        halos[far, c] = pair_exchange(columns[far, c], SX, far)
    columns, halos = [[table[far, c] for far in range(2) for c in range(2)] for table in (columns, halos)]
    modes = f32(2, 2, f, h)
    accum, send_even, send_odd, keep, give = call(
        functools.partial(last_batch_kernel, size, 1),
        [ext_type, columns_type, columns_type, modes, modes],
        (visit_order, offsets, *columns, *halos, grads, *fixed_args, amp),
        [SMEM] * 2 + [VMEM] * 10 + fixed_specs,
        [pltpu.VMEM(t.shape, t.dtype) for t in (ext_type, grads_type)] + batch_scratch(f),
        12 << 20,
    )

    x_got = pair_exchange(send_even, SX, 0), pair_exchange(send_odd, SX, 1, 1)
    strips = f32(2, 2, h, h)
    inner, *sent = call(functools.partial(fold_last_kernel, h), [f32(2, 2, 2 * h, h), strips, strips], (accum, *x_got))
    got = [pair_exchange(part, SY, odd) for odd, part in enumerate(sent)]
    out_re, out_im = call(
        functools.partial(finish_object_kernel, h), [f32(2 * h, 2 * h)] * 2, (scale, inner, *got, *columns)
    )

    first, block_bits, pairs = plan_bits()
    keep, give = keep.reshape(-1, h), give.reshape(-1, h)
    both = call(sum_kernel, f32(*keep.shape), (keep, flip_exchange(give, *first)))
    pieces = block_exchange(both, block_bits)
    total = call(sum_block_kernel, f32(keep.shape[0] >> len(block_bits), h), (pieces,))
    for at, (axis, bit) in enumerate(pairs):
        got = flip_exchange(total, axis, bit)
        last_pair = at == len(pairs) - 1
        kernel, shape = (spread_kernel, keep.shape) if last_pair else (sum_kernel, total.shape)
        total = call(kernel, f32(*shape), (total, got))
    total = block_exchange(total, block_bits)
    got = flip_exchange(total, *first)
    probe_rate = PROBE_GAIN / (positions * math.sqrt(lax.axis_size(SY) * lax.axis_size(SX)))
    piece = (2, 2, f, h)
    probe_out = call(
        functools.partial(finish_probe_kernel, probe_rate),
        [f32(2, f, f)] * 2,
        (total.reshape(piece), got.reshape(piece), *probe),
    )
    return (out_re, out_im, probe_out[0], probe_out[1])


def solution(mesh):
    return jax.shard_map(
        local,
        mesh=mesh,
        in_specs=(
            P(SY, SX),
            P(SY, SX),
            P(),
            P(),
            P(SY, SX, None, None, None),
            P(SY, SX, None, None),
            P(SY, SX, None),
        ),
        out_specs=(P(SY, SX), P(SY, SX), P(), P()),
        check_vma=False,
    )
```

```python
import functools
import math

import jax
import jax.numpy as jnp
from jax import lax
from jax.experimental import pallas as pl
from jax.experimental.pallas import tpu as pltpu
from jax.sharding import PartitionSpec as P

BATCHES = 2
SY, SX = "sy", "sx"

OBJECT_RATE = 0.25
PROBE_GAIN = 4.0

VMEM = pl.BlockSpec(memory_space=pltpu.VMEM)
SMEM = pl.BlockSpec(memory_space=pltpu.SMEM)
HBM = pl.BlockSpec(memory_space=pltpu.HBM)


def call(kernel, out_shape, operands, in_specs=None, scratch=(), room=0, out_spec=VMEM):
    outs = jax.tree.leaves(out_shape)
    specs = in_specs or [VMEM] * len(operands)
    held = [a for a, spec in zip(operands, specs) if spec is VMEM]
    need = sum(a.dtype.itemsize * math.prod(a.shape) for a in held + outs) + room
    return pl.pallas_call(
        kernel,
        out_shape=out_shape,
        in_specs=specs,
        out_specs=jax.tree.map(lambda _: out_spec, out_shape),
        scratch_shapes=scratch,
        compiler_params=pltpu.CompilerParams(vmem_limit_bytes=need + (1 << 20)),
    )(*operands)


def f32(*shape):
    return jax.ShapeDtypeStruct(shape, jnp.float32)


def prepare_kernel(
    order, order_hbm, offs_hbm, re_hbm, im_hbm, amp_hbm,
    table_left, table_right, scale, order_out, offs, probe_re, probe_im, amp, sems,
):
    f = probe_re.shape[1]
    moves = [(order_hbm, order_out), (offs_hbm, offs), (re_hbm, probe_re), (im_hbm, probe_im)]
    moves += [(amp_hbm.at[0, 0, order[0, 0, j]], amp.at[j]) for j in range(amp.shape[0])]
    copies = [pltpu.make_async_copy(a, b, sems.at[i]) for i, (a, b) in enumerate(moves)]
    for copy in copies:
        copy.start()
    rows = lax.broadcasted_iota(jnp.int32, (f, f), 0)
    cols = lax.broadcasted_iota(jnp.int32, (f, f), 1)
    phase_angle = 2.0 * math.pi / f * lax.rem(rows * cols, f).astype(jnp.float32)
    norm_scale = 1.0 / math.sqrt(f)
    table_re = (jnp.cos(phase_angle) * norm_scale).astype(jnp.bfloat16)
    table_im = (-jnp.sin(phase_angle) * norm_scale).astype(jnp.bfloat16)
    for table, sign in ((table_left, 1), (table_right, -1)):
        table[:f, :f] = table_re
        table[f:, f:] = table_re
        table[:f, f:] = table_im if sign < 0 else -table_im
        table[f:, :f] = table_im if sign > 0 else -table_im
    for copy in copies:
        copy.wait()
    power = sum(part[m] * part[m] for part in (probe_re, probe_im) for m in range(2))
    scale[...] = OBJECT_RATE / jnp.broadcast_to(jnp.max(power), scale.shape)


def pair_exchange(block, axis, odd, bit=2):
    count_y, count_x = lax.axis_size(SY), lax.axis_size(SX)
    perm = []
    for y in range(count_y):
        for x in range(count_x):
            index, count = (y, count_y) if axis == SY else (x, count_x)
            partner = index + 1 if index % 2 == odd else index - 1
            if 0 <= partner < count:
                to_y, to_x = (partner, x) if axis == SY else (y, partner)
            else:
                to_y, to_x = (y, stand_in(x, count_x, bit)) if axis == SY else (stand_in(y, count_y, bit), x)
            perm.append((y * count_x + x, to_y * count_x + to_x))
    return lax.ppermute(block, (SY, SX), perm)


def stand_in(index, count, bit):
    other = index ^ bit
    return other if other < count else index


def has_partner(axis, odd):
    index, count = lax.axis_index(axis), lax.axis_size(axis)
    partner = jnp.where(lax.rem(index, 2) == odd, index + 1, index - 1)
    return (partner >= 0) & (partner < count)


def masked(axis, odd, block):
    return jnp.where(has_partner(axis, odd), block, 0.0)


def parity(axis):
    return lax.rem(lax.axis_index(axis), 2)


def aligned(value, unit):
    return pl.multiple_of(value, unit)


def run_copies(pairs, sems):
    copies = [pltpu.make_async_copy(a, b, sems.at[i]) for i, (a, b) in enumerate(pairs)]
    for copy in copies:
        copy.start()
    for copy in copies:
        copy.wait()


def lane_block(far):
    px = parity(SX)
    return px if far else 1 - px


def pack_rows_kernel(h, obj_re, obj_im, *outs_and_sems):
    *outs, sems = outs_and_sems
    py = parity(SY)
    pairs = []
    for at, out in enumerate(outs):
        far, odd = divmod(at, 2)
        rows = pl.ds(aligned((py if odd else 1 - py) * h, h), h)
        columns = pl.ds(aligned(lane_block(far) * h, h), h)
        pairs += [(obj.at[rows, columns], out.at[c]) for c, obj in enumerate((obj_re, obj_im))]
    run_copies(pairs, sems)


def pack_columns_kernel(h, obj_re, obj_im, x_even, x_odd, tile, sems):
    px = parity(SX)
    pairs = []
    for c, obj in enumerate((obj_re, obj_im)):
        for out, side in ((x_even, 1 - px), (x_odd, px)):
            pairs.append((obj.at[:, pl.ds(aligned(side * h, h), h)], out.at[c]))
        pairs += [(obj.at[:, pl.ds(lb * h, h)], tile.at[c, lb]) for lb in range(2)]
    run_copies(pairs, sems)


def pack_corner_kernel(up_even, up_odd, corner):
    for odd, strip in enumerate((up_even, up_odd)):
        corner[odd] = masked(SY, odd, strip[...])


def batch_body(
    batch, size, order, offs, probe, tables, amp, ext, accum, grads, grads_before, scratch
):
    sets = [scratch[i::2] for i in range(2)]
    f = probe[0].shape[1]
    h = f // 2
    rows = 16
    lane = lax.broadcasted_iota(jnp.int32, (rows, h), 1)
    table_left, table_right = tables

    def place(j):
        chosen = order[0, 0, batch * size + j]
        left = offs[0, 0, 1, chosen] + h
        return offs[0, 0, 0, chosen] + h, lax.div(left, h), lax.rem(left, h)

    def exits_of(j):
        patch, exits, *_ = sets[j % 2]
        top, first, shift = place(j)
        back_shift = lax.rem(h - shift, h)
        inside = lane < h - shift
        for r in range(0, f, rows):
            here = pl.ds(r, rows)
            window = []
            for c in range(2):
                a, b, d = [
                    pltpu.roll(ext[c, first + k, pl.ds(top + r, rows), :], back_shift, 1) for k in range(3)
                ]
                window.append([jnp.where(inside, a, b), jnp.where(inside, b, d)])
            for lb in range(2):
                o_re, o_im = window[0][lb], window[1][lb]
                patch[0, here, pl.ds(lb * h, h)] = o_re
                patch[1, here, pl.ds(lb * h, h)] = o_im
                for m in range(2):
                    p_re, p_im = [part[m, here, pl.ds(lb * h, h)] for part in probe]
                    spot = pl.ds(m * f + lb * h, h)
                    exits[pl.ds(r, rows), spot] = (p_re * o_re - p_im * o_im).astype(jnp.bfloat16)
                    exits[pl.ds(f + r, rows), spot] = (p_re * o_im + p_im * o_re).astype(jnp.bfloat16)

    def transform(j, values, first_table, second_table):
        mixed, field = sets[j % 2][3:]
        product = jnp.dot(first_table[...], values[...], preferred_element_type=jnp.float32)
        for c in range(2):
            for m in range(2):
                part = product[c * f : (c + 1) * f, m * f : (m + 1) * f]
                mixed[pl.ds(m * f, f), pl.ds(c * f, f)] = part.astype(jnp.bfloat16)
        field[...] = jnp.dot(mixed[...], second_table[...], preferred_element_type=jnp.float32)

    def forward(j):
        transform(j, sets[j % 2][1], table_left, table_right)

    def backward(j):
        transform(j, sets[j % 2][2], table_right, table_left)

    def correct(j):
        _, _, fixed, _, field = sets[j % 2]
        for r in range(0, f, rows):
            for lb in range(2):
                far = [
                    [field[pl.ds(m * f + r, rows), pl.ds(c * f + lb * h, h)] for c in range(2)] for m in range(2)
                ]
                power = sum(part * part for mode in far for part in mode)
                ratio = amp[batch * size + j, pl.ds(r, rows), pl.ds(lb * h, h)] * lax.rsqrt(jnp.maximum(power, 1.0))
                for m in range(2):
                    for c in range(2):
                        spot = pl.ds(m * f + lb * h, h)
                        fixed[pl.ds(c * f + r, rows), spot] = (far[m][c] * ratio).astype(jnp.bfloat16)

    def gradients(j):
        patch, exits, _, _, field = sets[j % 2]
        top, first, shift = place(j)
        beyond = lane >= shift
        for r in range(0, f, rows):
            here = pl.ds(r, rows)
            term = [[0.0, 0.0], [0.0, 0.0]]
            for lb in range(2):
                cols = pl.ds(lb * h, h)
                o_re, o_im = patch[0, here, cols], patch[1, here, cols]
                for m in range(2):
                    d_re, d_im = [
                        field[pl.ds(m * f + r, rows), pl.ds(c * f + lb * h, h)]
                        - exits[pl.ds(c * f + r, rows), pl.ds(m * f + lb * h, h)].astype(jnp.float32)
                        for c in range(2)
                    ]
                    p_re, p_im = [part[m, here, cols] for part in probe]
                    term[0][lb] += p_re * d_re + p_im * d_im
                    term[1][lb] += p_re * d_im - p_im * d_re
                    for c, part in enumerate((o_re * d_re + o_im * d_im, o_re * d_im - o_im * d_re)):
                        sofar = grads if j else grads_before
                        grads[m, c, lb, here, :] = part if sofar is None else sofar[m, c, lb, here, :] + part
            for c in range(2):
                a, b = [pltpu.roll(part, shift, 1) for part in term[c]]
                there = pl.ds(top + r, rows)
                accum[c, first, there, :] += jnp.where(beyond, a, 0.0)
                accum[c, first + 1, there, :] += jnp.where(beyond, b, a)
                accum[c, first + 2, there, :] += jnp.where(beyond, 0.0, b)

    exits_of(0)
    for j in range(0, size, 2):
        pair = j + 1 < size
        forward(j)
        if j == 0:
            accum[...] = jnp.zeros_like(accum)
        else:
            gradients(j - 1)
        if pair:
            exits_of(j + 1)
            forward(j + 1)
        correct(j)
        backward(j)
        if pair:
            correct(j + 1)
            backward(j + 1)
        gradients(j)
        if j + 2 < size:
            exits_of(j + 2)
        elif pair:
            gradients(j + 1)


def first_batch_kernel(
    h, size, order, offs, tile, up_00, up_01, up_10, up_11, x_even, x_odd, c_even, c_odd,
    probe_re, probe_im, table_left, table_right, amp,
    ext, accum, send_even, send_odd_re, send_odd_im, grads, *scratch,
):
    py, px = parity(SY), parity(SX)
    halo_rows = [pl.ds(aligned(side * 3 * h, h), h) for side in (1 - py, py)]
    ups = ((up_00, up_01), (up_10, up_11))
    for c in range(2):
        for lb in range(2):
            ext[c, 1 + lb, h : 3 * h] = tile[c, lb]
        for far, (block, column, corner) in enumerate((((1 - px) * 3, x_even, c_even), (px * 3, x_odd, c_odd))):
            ext[c, block, h : 3 * h] = masked(SX, far, column[c])
            for odd in range(2):
                ext[c, 1 + lane_block(far), halo_rows[odd]] = masked(SY, odd, ups[far][odd][c])
                ext[c, block, halo_rows[odd]] = masked(SX, far, corner[odd, c])
    probe, tables = (probe_re, probe_im), (table_left, table_right)
    batch_body(0, size, order, offs, probe, tables, amp, ext, accum, grads, None, scratch)
    for c, send_odd in enumerate((send_odd_re, send_odd_im)):
        send_even[c] = accum[c, (1 - px) * 3]
        send_odd[...] = accum[c, px * 3]


def last_batch_kernel(
    size, batch, order, offs, near_re, near_im, far_re, far_im, even_re, even_im, odd_re, odd_im, grads_in,
    probe_re, probe_im, table_left, table_right, amp, accum, send_even, send_odd, keep, give, ext, grads, *scratch,
):
    px = parity(SX)
    for c, parts in enumerate(((near_re, far_re, even_re, odd_re), (near_im, far_im, even_im, odd_im))):
        near, far, x_even, x_odd = parts
        ext[c, 1 + lane_block(0)] = near[...]
        ext[c, 1 + lane_block(1)] = far[...]
        ext[c, (1 - px) * 3] = masked(SX, 0, x_even[...])
        ext[c, px * 3] = masked(SX, 1, x_odd[...])
    probe, tables = (probe_re, probe_im), (table_left, table_right)
    batch_body(batch, size, order, offs, probe, tables, amp, ext, accum, grads, grads_in, scratch)
    keep[...] = grads[px]
    give[...] = grads[1 - px]
    for c in range(2):
        send_even[c] = accum[c, (1 - px) * 3]
        send_odd[c] = accum[c, px * 3]


def batch_scratch(f):
    flat = [pltpu.VMEM((2 * f, 2 * f), dtype) for dtype in (jnp.bfloat16,) * 3 + (jnp.float32,)]
    each = [pltpu.VMEM((2, f, f), jnp.float32), *flat]
    return [buffer for buffer in each for _ in range(2)]


def half_side(odd):
    py = parity(SY)
    return py if odd else 1 - py


def half_rows(h, odd):
    return pl.ds(aligned(half_side(odd) * 2 * h, 2 * h), 2 * h)


def fold_columns_kernel(h, c, far, accum, x_got, y_even, y_odd):
    for odd, y_send in enumerate((y_even, y_odd)):
        rows = half_rows(h, odd)
        column = x_got[rows] if far else x_got[c, rows]
        y_send[...] = accum[c, 1 + lane_block(far), rows] + masked(SX, far, column)


def update_kernel(h, c, far, scale, sent_even, got_even, sent_odd, got_odd, ext, columns):
    rate = scale[0:1, :]
    for odd, sent, got in ((0, sent_even, got_even), (1, sent_odd, got_odd)):
        side = half_side(odd)
        rate_halo = jnp.where(has_partner(SY, odd), rate, 0.0)
        for at, factor in ((1 - side, rate), (side, rate_halo)):
            here = pl.ds(aligned(at * h, h), h)
            there = pl.ds(aligned((2 * side + at) * h, h), h)
            total = sent[here] + masked(SY, odd, got[here])
            columns[there] = ext[c, 1 + lane_block(far), there] + factor * total


def fold_last_kernel(h, accum, x_even, x_odd, inner, y_even, y_odd):
    py = parity(SY)
    for far, x_got in enumerate((x_even, x_odd)):
        for c in range(2):
            total = accum[c, 1 + lane_block(far)] + masked(SX, far, x_got[c])
            inner[far, c] = total[h : 3 * h]
            y_even[far, c] = jnp.where(py == 0, total[3 * h :], total[:h])
            y_odd[far, c] = jnp.where(py == 0, total[:h], total[3 * h :])


def finish_object_kernel(h, scale, inner, y_even, y_odd, near_re, near_im, far_re, far_im, *outs):
    columns = (near_re, near_im), (far_re, far_im)
    rate = scale[0:1, :]
    for far in range(2):
        lanes = pl.ds(aligned(lane_block(far) * h, h), h)
        for c, out in enumerate(outs):
            for odd, got in enumerate((y_even, y_odd)):
                side = half_side(odd)
                here = pl.ds(aligned(side * h, h), h)
                old = columns[far][c][pl.ds(aligned((1 + side) * h, h), h)]
                out[here, lanes] = old + rate * (inner[far, c, here] + masked(SY, odd, got[far, c]))


def plan_bits():
    bits = {axis: lax.axis_size(axis).bit_length() - 1 for axis in (SY, SX)}
    for axis, count in bits.items():
        if 1 << count != lax.axis_size(axis):
            raise ValueError("axis size")
    first, *across = [(SX, bit) for bit in range(bits[SX])]
    along = [(SY, bit) for bit in range(bits[SY])]
    block = along[:2] + across[:1]
    return first, block, along[2:] + across[1:]


def flip_exchange(block, axis, bit):
    count_y, count_x = lax.axis_size(SY), lax.axis_size(SX)
    flip_y, flip_x = (1 << bit, 0) if axis == SY else (0, 1 << bit)
    perm = [(y * count_x + x, (y ^ flip_y) * count_x + (x ^ flip_x)) for y in range(count_y) for x in range(count_x)]
    return lax.ppermute(block, (SY, SX), perm)


def block_exchange(pieces, bits):
    count_y, count_x = lax.axis_size(SY), lax.axis_size(SX)
    mask_y, mask_x = [sum(1 << bit for axis, bit in bits if axis == own) for own in (SY, SX)]
    groups = {}
    for y in range(count_y):
        for x in range(count_x):
            groups.setdefault((y & ~mask_y, x & ~mask_x), []).append(y * count_x + x)
    return lax.all_to_all(pieces, (SY, SX), 0, 0, tiled=True, axis_index_groups=list(groups.values()))


def sum_kernel(left, right, out):
    out[...] = left[...] + right[...]


def sum_block_kernel(pieces, out):
    size = out.shape[0]
    out[...] = sum(pieces[at : at + size, :] for at in range(0, pieces.shape[0], size))


def spread_kernel(left, right, out):
    total = left[...] + right[...]
    size = total.shape[0]
    for at in range(0, out.shape[0], size):
        out[at : at + size, :] = total


def finish_probe_kernel(rate, keep, got, probe_re, probe_im, out_re, out_im, done, sems):
    px = parity(SX)
    h = probe_re.shape[1] // 2
    copies = []
    for at, (mode, part) in enumerate(((px, keep), (1 - px, got))):
        for c, (probe, out) in enumerate(((probe_re, out_re), (probe_im, out_im))):
            spot = 2 * at + c
            for lb in range(2):
                cols = slice(lb * h, (lb + 1) * h)
                done[spot, :, cols] = probe[mode, :, cols] + rate * part[c, lb]
            copies.append(pltpu.make_async_copy(done.at[spot], out.at[mode], sems.at[spot]))
            copies[spot].start()
    for copy in copies:
        copy.wait()


def local(object_re, object_im, probe_re, probe_im, amplitudes, offsets, visit_order):
    f = probe_re.shape[1]
    h = f // 2
    positions = visit_order.shape[-1]
    size = positions // BATCHES
    table_type = jax.ShapeDtypeStruct((2 * f, 2 * f), jnp.bfloat16)
    in_hbm = functools.partial(pltpu.with_memory_space_constraint, memory_space=pltpu.HBM)
    offsets = offsets.transpose(0, 1, 3, 2)
    arrays = (visit_order, offsets, probe_re, probe_im)
    table_left, table_right, scale, *arrays, amp = call(
        prepare_kernel,
        [table_type, table_type, f32(8, h)] + [jax.ShapeDtypeStruct(a.shape, a.dtype) for a in arrays] + [f32(positions, f, f)],
        (visit_order, *map(in_hbm, arrays), in_hbm(amplitudes)),
        [SMEM] + [HBM] * 5,
        [pltpu.SemaphoreType.DMA((4 + positions,))],
    )
    visit_order, offsets, *probe = arrays
    strip = f32(2, h, h)
    block = f32(2, 2 * h, h)
    objects = in_hbm(object_re), in_hbm(object_im)
    sems = [pltpu.SemaphoreType.DMA((8,))]
    up = call(functools.partial(pack_rows_kernel, h), [strip] * 4, objects, [HBM] * 2, sems)
    x_even, x_odd, tile = call(
        functools.partial(pack_columns_kernel, h), [block, block, f32(2, 2, 2 * h, h)], objects, [HBM] * 2, sems
    )
    ups = {}
    for far in (1, 0):
        ups[far] = [pair_exchange(up[2 * far + odd], SY, odd) for odd in range(2)]
    x_even = pair_exchange(x_even, SX, 0)
    x_odd = pair_exchange(x_odd, SX, 1)
    corners = [pair_exchange(call(pack_corner_kernel, f32(2, 2, h, h), ups[far]), SX, far) for far in range(2)]

    column, columns_type = f32(4 * h, h), f32(2, 4 * h, h)
    ext_type, grads_type = f32(2, 4, 4 * h, h), f32(2, 2, 2, f, h)
    fixed_args = (*probe, table_left, table_right)
    fixed_specs = [VMEM] * 4
    ext, accum, send_even, *send_odd, grads = call(
        functools.partial(first_batch_kernel, h, size),
        [ext_type, ext_type, columns_type, column, column, grads_type],
        (visit_order, offsets, tile, *ups[0], *ups[1], x_even, x_odd, *corners, *fixed_args, amp),
        [SMEM] * 2 + [VMEM] * 10 + fixed_specs,
        batch_scratch(f),
        9 << 20,
    )

    half = f32(2 * h, h)
    x_even = pair_exchange(send_even, SX, 0)
    x_odd = [pair_exchange(part, SX, 1) for part in send_odd]
    columns, halos = {}, {}
    for far, c in ((0, 0), (1, 0), (1, 1), (0, 1)):
        sent = call(
            functools.partial(fold_columns_kernel, h, c, far), [half, half], (accum, x_odd[c] if far else x_even)
        )
        got = [pair_exchange(part, SY, odd) for odd, part in enumerate(sent)]
        columns[far, c] = call(
            functools.partial(update_kernel, h, c, far), column, (scale, sent[0], got[0], sent[1], got[1], ext)
        )
        halos[far, c] = pair_exchange(columns[far, c], SX, far)
    columns, halos = [[table[far, c] for far in range(2) for c in range(2)] for table in (columns, halos)]
    modes = f32(2, 2, f, h)
    accum, send_even, send_odd, keep, give = call(
        functools.partial(last_batch_kernel, size, 1),
        [ext_type, columns_type, columns_type, modes, modes],
        (visit_order, offsets, *columns, *halos, grads, *fixed_args, amp),
        [SMEM] * 2 + [VMEM] * 10 + fixed_specs,
        [pltpu.VMEM(t.shape, t.dtype) for t in (ext_type, grads_type)] + batch_scratch(f),
        12 << 20,
    )

    x_got = pair_exchange(send_even, SX, 0), pair_exchange(send_odd, SX, 1, 1)
    strips = f32(2, 2, h, h)
    inner, *sent = call(functools.partial(fold_last_kernel, h), [f32(2, 2, 2 * h, h), strips, strips], (accum, *x_got))
    got = [pair_exchange(part, SY, odd) for odd, part in enumerate(sent)]
    out_re, out_im = call(
        functools.partial(finish_object_kernel, h), [f32(2 * h, 2 * h)] * 2, (scale, inner, *got, *columns)
    )

    first, block_bits, pairs = plan_bits()
    keep, give = keep.reshape(-1, h), give.reshape(-1, h)
    both = call(sum_kernel, f32(*keep.shape), (keep, flip_exchange(give, *first)))
    pieces = block_exchange(both, block_bits)
    total = call(sum_block_kernel, f32(keep.shape[0] >> len(block_bits), h), (pieces,))
    for at, (axis, bit) in enumerate(pairs):
        got = flip_exchange(total, axis, bit)
        last_pair = at == len(pairs) - 1
        kernel, shape = (spread_kernel, keep.shape) if last_pair else (sum_kernel, total.shape)
        total = call(kernel, f32(*shape), (total, got))
    total = block_exchange(total, block_bits)
    got = flip_exchange(total, *first)
    probe_rate = PROBE_GAIN / (positions * math.sqrt(lax.axis_size(SY) * lax.axis_size(SX)))
    piece = (2, 2, f, h)
    probe_out = call(
        functools.partial(finish_probe_kernel, probe_rate),
        [f32(2, f, f)] * 2,
        (total.reshape(piece), got.reshape(piece), *probe),
        scratch=[pltpu.VMEM((4, f, f), jnp.float32), pltpu.SemaphoreType.DMA((4,))],
        out_spec=HBM,
    )
    return (out_re, out_im, probe_out[0], probe_out[1])


def solution(mesh):
    return jax.shard_map(
        local,
        mesh=mesh,
        in_specs=(
            P(SY, SX),
            P(SY, SX),
            P(),
            P(),
            P(SY, SX, None, None, None),
            P(SY, SX, None, None),
            P(SY, SX, None),
        ),
        out_specs=(P(SY, SX), P(SY, SX), P(), P()),
        check_vma=False,
    )
```
